256 devices in a mesh: dp: 4 (over x_lo, core), expert: 64 (over x_hi, y, z).
Axes of the slice: x: 4 (x_hi: 2, x_lo: 2; x = x_hi * 2 + x_lo), y: 4, z: 8, core: 2. Of those that a mesh axis runs over, the one named last changes fastest.
Arguments:
- tokens: bfloat16 [16384, 4096], P(('dp', 'expert')), may hold values from -6 to 6
- token_experts: int32 [16384, 8], P(('dp', 'expert')), may hold values from 0 to 63, all different within a row; in each aligned block of 64 rows (0 to 63, 64 to 127, ...) at most 12 rows name the same one
- hidden_grad: bfloat16 [16384, 8, 768], P(('dp', 'expert')), may hold values from -6 to 6
- held_expert: int32 [64], replicated, may hold values from 0 to 63, each once
- swap_mask: int32 [64], replicated, may hold values from 0 to 1, as said below
- weight: bfloat16 [64, 4096, 768], P('expert', 'dp'), may hold values from -0.09375 to 0.09375
- first_moment: float32 [64, 4096, 768], P('expert', 'dp'), may hold values from -81.4587 to 81.4587
- second_moment: float32 [64, 4096, 768], P('expert', 'dp'), may hold values from 20.48 to 204.8
Outputs:
- token_grad: bfloat16 [16384, 4096], P(('dp', 'expert'))
- adam_step: bfloat16 [64, 4096, 768], P('expert', 'dp')
The draws below stay inside these ranges and needn't reach their ends.
Inputs may be any that keep to these rules, and one draw needn't show every extreme that they name: `token_experts`: in each aligned block of 64 rows (the tokens of one device) no expert is named by more than 12 rows, and in some blocks one is named by exactly 12; the ids of a row differ. `held_expert`: a permutation of the expert ids. swap_mask[p] equals swap_mask[p + 32] for p below 32, and exactly 8 such pairs are 1.
All inputs are finite; a program needn't handle non-finite values.
Results may differ from the reference program's by a relative error of at most 0.008.
Values may be sent and summed in bfloat16 or wider, within the bound.
No kernel may reach another device: no remote copies, remote signals or barrier semaphores. Data moves between devices by JAX's collectives and lax.ppermute only.
A program may use at most 128 MiB of HBM per device.

```python
import math
import jax
import jax.numpy as jnp
import numpy as np
from jax import lax

D = 4096
FF = 768
TOP = 8
TOK_DEV = 64
EXPERTS = 64
TOKENS = 16384
REPLICA_TOKENS = 4096
CAP = 12
SLOTS = 768
ROWS_EXPERT = 2048
SWAP_PAIRS = 8
N_DP = 4


def draw_swap_mask(key, part):
    half_count = EXPERTS // 2
    order = jax.random.permutation(key, half_count)
    lower = (order < SWAP_PAIRS).astype(jnp.int32)
    return jnp.concatenate([lower, lower])


def levels(key, dims, pieces, smallest, largest):
    def one(dim, shards_of):
        steps = jax.random.uniform(jax.random.fold_in(jax.random.fold_in(key, 6), dim), (shards_of,), jnp.float32, smallest / len(pieces), largest / len(pieces))
        return jnp.repeat(jnp.exp(steps), dims[dim] // shards_of).reshape((-1,) + (1,) * (len(dims) - dim - 1))

    gain = one(*pieces[0])
    for cut in pieces[1:]:
        gain = gain * one(*cut)
    return gain


def shared_out(own_key, own, number, rows, count, top, reach, slope):
    sequence = jax.random.permutation(own_key, count)
    crowded, common = shares(count, rows * top, reach, slope, True), shares(count, rows * top, reach, slope, False)
    places = jnp.arange(count)

    def named(tallies, rotation):
        used = int((tallies > 0).sum())
        fixed = max(1, used // 4)
        passed = fixed + (places - fixed + rotation * (used - fixed)) % max(1, count - fixed)
        return jnp.zeros((count,), jnp.int32).at[sequence[jnp.where(places < fixed, places, passed)]].set(jnp.asarray(tallies, jnp.int32))

    tallies = jnp.where(number % 4 == 0, named(crowded, number // 4), named(common, number - number // 4 - 1))
    mixed = jax.random.permutation(jax.random.fold_in(own, 3), count)
    donor, sink = mixed[0:count // 2 * 2:2], mixed[1:count // 2 * 2:2]
    margin = jnp.minimum(tallies[donor] - 1, reach - tallies[sink]) // 2
    margin = jnp.where((donor == sequence[0]) | (sink == sequence[0]) | (tallies[sink] == 0), 0, jnp.maximum(margin, 0))
    passed = jax.random.randint(jax.random.fold_in(own, 4), (count // 2,), 0, 1 << 20) % (margin + 1)
    tallies = tallies.at[donor].add(-passed).at[sink].add(passed)
    items = jnp.searchsorted(jnp.cumsum(tallies), jnp.arange(rows * top), side="right").astype(jnp.int32)
    table = items.reshape(top, rows).T
    table = table[jax.random.permutation(jax.random.fold_in(own, 1), rows)]
    rotation = jax.random.randint(jax.random.fold_in(own, 2), (rows, 1), 0, top)
    return jnp.take_along_axis(table, (jnp.arange(top)[None, :] + rotation) % top, axis=1)


def shares(count, total, limit, slope, full):
    portions = [(1 << 20) // math.isqrt(standing ** slope) + 1 for standing in range(1, count + 1)]
    largest = limit if full else min(limit, max(-(-total // count), total * portions[0] // sum(portions)))
    least = 1 if total - largest >= count - 1 else 0
    counts, rest = [largest] + [least] * (count - 1), total - largest - least * (count - 1)
    while rest > 0:
        movable = [i for i in range(1, count) if counts[i] < largest] or [i for i in range(1, count) if counts[i] < limit]
        whole, left = sum([portions[i] for i in movable]), rest
        for i in movable:
            addition = min(limit - counts[i], max(1, left * portions[i] // whole), rest)
            counts[i] = counts[i] + addition
            rest = rest - addition
    return np.array(counts)


def gaussian(rng, extent, spread, reach, split=(), kind=jnp.bfloat16):
    array = jax.random.normal(rng, extent, jnp.float32) * spread
    if len(split) > 0:
        array = levels(rng, extent, split, -0.22, 0.18) * array
    return jnp.clip(array, min=-reach, max=reach).astype(kind)


def setup_inputs(seed: int = 0) -> dict:
    seeds = jax.random.split(jax.random.key(seed), 9)
    tokens = gaussian(seeds[0], (TOKENS, D), 1.0, 6.0, ((0, 256),))
    token_experts_keys = jax.random.split(jax.random.fold_in(seeds[1], 1), TOKENS // TOK_DEV)
    token_experts_turns = jax.random.permutation(jax.random.fold_in(seeds[1], 3), TOKENS // TOK_DEV)
    token_experts = jax.vmap(lambda own, number: shared_out(jax.random.fold_in(seeds[1], 2), own, number, TOK_DEV, EXPERTS, TOP, CAP, 2))(token_experts_keys, token_experts_turns).reshape((TOKENS, TOP))
    hidden_grad = gaussian(seeds[2], (TOKENS, TOP, FF), 1.0, 6.0, ((0, 256),))
    held_expert = jax.random.permutation(seeds[3], EXPERTS).astype(jnp.int32)
    swap_mask = draw_swap_mask(jax.random.fold_in(seeds[8], 71), 0)
    weight = gaussian(seeds[5], (EXPERTS, D, FF), D ** -0.5, 0.09375, ((0, 64), (1, 4)))
    first_moment = gaussian(seeds[6], (EXPERTS, D, FF), (0.3 * ROWS_EXPERT ** 0.5), 81.4587, ((0, 64), (1, 4)), jnp.float32)
    second_moment = jnp.clip(jnp.exp(math.log(204.8) - 2.3025851 * jax.random.uniform(seeds[7], (EXPERTS, D, FF), jnp.float32) ** levels(seeds[7], (EXPERTS, D, FF), ((0, 64), (1, 4)), -0.2, 0.2)), 20.48, 204.8)
    return {"tokens": tokens, "token_experts": token_experts, "hidden_grad": hidden_grad, "held_expert": held_expert, "swap_mask": swap_mask, "weight": weight, "first_moment": first_moment, "second_moment": second_moment}


def adam_direction(grad, first, second):
    first_new = 0.9 * first + 0.1 * grad
    second_new = 0.95 * second + 0.05 * grad * grad
    return (first_new / (jnp.sqrt(second_new) + 1e-08)).astype(jnp.bfloat16)

def reference(tokens, token_experts, hidden_grad, held_expert, swap_mask, weight, first_moment, second_moment):
    lanes = jnp.arange(EXPERTS, dtype=jnp.int32)
    partner = (lanes + EXPERTS // 2) % EXPERTS
    source_slot = jnp.where(swap_mask == 1, partner, lanes).astype(jnp.int32)
    new_held = held_expert[source_slot]
    slot_of = lax.optimization_barrier(jnp.sum(jnp.where(held_expert[None, :] == lanes[:, None], lanes[None, :], 0), axis=1)).astype(jnp.int32)
    width = tokens.shape[1]
    hidden = hidden_grad.shape[2]
    top = token_experts.shape[1]
    rep_tokens = tokens.reshape(N_DP, REPLICA_TOKENS, width)
    rep_ids = token_experts.reshape(N_DP, REPLICA_TOKENS, top)
    rep_grads = hidden_grad.reshape(N_DP, REPLICA_TOKENS, top, hidden)
    picks = jnp.arange(top, dtype=jnp.int32)
    slot_range = jnp.arange(SLOTS, dtype=jnp.int32)

    def step(carry, lane):
        expert_id = new_held[lane]
        full_w = weight[slot_of[expert_id]]
        total = jnp.zeros((width, hidden), jnp.float32)
        for rep in range(N_DP):
            hit_k = rep_ids[rep] == expert_id
            hit = jnp.any(hit_k, axis=1)
            kpos = lax.optimization_barrier(jnp.sum(jnp.where(hit_k, picks[None, :], 0), axis=1)).astype(jnp.int32)
            rows = jnp.nonzero(hit, size=SLOTS, fill_value=0)[0].astype(jnp.int32)
            count = jnp.sum(hit.astype(jnp.int32))
            valid = slot_range < count
            xs = rep_tokens[rep][rows]
            gs = rep_grads[rep][rows, kpos[rows]]
            gs = jnp.where(valid[:, None], gs, jnp.zeros_like(gs))
            pre = jnp.dot(xs, full_w, preferred_element_type=jnp.float32)
            sig = jax.nn.sigmoid(pre)
            grad_pre = (gs.astype(jnp.float32) * sig * (1.0 + pre * (1.0 - sig))).astype(jnp.bfloat16)
            row_grad = jnp.dot(grad_pre, full_w.T, preferred_element_type=jnp.float32).astype(jnp.bfloat16)
            carry = carry.at[rep, rows].add(row_grad.astype(jnp.float32))
            part = lax.dot_general(xs, grad_pre, (((0,), (0,)), ((), ())), preferred_element_type=jnp.float32)
            part = lax.optimization_barrier(part.astype(jnp.bfloat16))
            total = total + part.astype(jnp.float32)
        src = source_slot[lane]
        return (carry, adam_direction(total, first_moment[src], second_moment[src]))
    start = jnp.zeros((N_DP, REPLICA_TOKENS, width), jnp.float32)
    carry, adam_step = lax.scan(step, start, lanes)
    token_grad = carry.reshape(N_DP * REPLICA_TOKENS, width).astype(jnp.bfloat16)
    return (token_grad, adam_step)
```

```python
import jax
import jax.numpy as jnp
from jax import lax
from jax.sharding import Mesh, PartitionSpec as P

CHUNKS = 2
SWAP_PARTS = 2


def adam_direction(grad, first, second):
    first_new = 0.9 * first + 0.1 * grad
    second_new = 0.95 * second + 0.05 * grad * grad
    return (first_new / (jnp.sqrt(second_new) + 1e-08)).astype(jnp.bfloat16)


def dot(a, b, contract=((1,), (0,))):
    return lax.dot_general(a, b, (contract, ((), ())), preferred_element_type=jnp.float32)


def flipped_groups(with_z):
    nz = 8 if with_z else 1
    return [
        [
            (((low ^ high) * 2 + high) * 4 + y) * nz + z
            for high in range(2)
            for y in range(4)
            for z in range(nz)
        ]
        for low in range(2)
    ]


def exchange_plane(block):
    return lax.all_to_all(
        block, ("xl", "xh", "y"), 0, 0, axis_index_groups=flipped_groups(False), tiled=True
    )


def exchange_all(block):
    return lax.all_to_all(
        block, ("xl", "xh", "y", "z"), 0, 0, axis_index_groups=flipped_groups(True), tiled=True
    )


def swapped(block, axis):
    return lax.ppermute(block, axis, [(0, 1), (1, 0)])


def step(
    tokens, token_experts, hidden_grad, held_expert, swap_mask, weight, first_moment, second_moment
):
    bf16, f32, i32 = jnp.bfloat16, jnp.float32, jnp.int32
    xl, core, xh = lax.axis_index("xl"), lax.axis_index("core"), lax.axis_index("xh")
    y, z = lax.axis_index("y"), lax.axis_index("z")
    here = (xh * 4 + y) * 8 + z
    tok_dev, top = token_experts.shape
    width, hidden = tokens.shape[1], hidden_grad.shape[2]
    slots = held_expert.shape[0]
    cap = 12
    planes, lanes_of_plane = 8, 8
    col = planes * tok_dev
    block = planes * cap
    rows = lanes_of_plane * block
    part = width // CHUNKS

    w_own = weight[0]
    w_x = swapped(w_own, "xl")
    w_c = swapped(w_own, "core")
    w_xc = swapped(w_x, "core")
    me = xl * 2 + core
    shard = w_own.shape[0]
    full_w = jnp.zeros((width, hidden), bf16)
    for piece, at in ((w_own, me), (w_c, me ^ 1), (w_x, me ^ 2), (w_xc, me ^ 3)):
        full_w = lax.dynamic_update_slice(full_w, piece, (at * shard, 0))

    same = token_experts[:, :, None] == held_expert[None, None, :]
    named = jnp.sum(same.astype(f32), axis=1).astype(bf16)
    earlier = (
        lax.broadcasted_iota(i32, (tok_dev, tok_dev), 1)
        < lax.broadcasted_iota(i32, (tok_dev, tok_dev), 0)
    ).astype(bf16)
    rank = named.astype(f32) * (dot(earlier, named) + 1.0)

    marks = jnp.pad(rank.astype(bf16), ((0, 0), (0, 128 - slots)))
    gathered = []
    for c in range(CHUNKS):
        piece = tokens[:, c * part : (c + 1) * part]
        if c == 0:
            piece = jnp.concatenate([piece, marks], axis=1)
        gathered.append(lax.all_gather(piece, "z", axis=0, tiled=True))

    place = jnp.arange(slots, dtype=f32) * cap - 1.0
    slot = jnp.sum(jnp.where(same, (rank + place[None, :])[:, None, :], 0.0), axis=2)
    slot = slot.astype(i32).reshape(1, tok_dev * top)
    pick_g = (lax.broadcasted_iota(i32, (slots * cap, tok_dev * top), 0) == slot).astype(bf16)
    send_g = dot(pick_g, hidden_grad.reshape(tok_dev * top, hidden)).astype(bf16)
    rows_g = exchange_all(send_g.reshape(slots, cap, hidden))
    rows_g = rows_g.reshape(rows, hidden)

    marks_col = gathered[0][:, part : part + slots]
    lane_i = lax.broadcasted_iota(i32, (lanes_of_plane, slots), 0)
    slot_i = lax.broadcasted_iota(i32, (lanes_of_plane, slots), 1)
    choose = (slot_i == lane_i * planes + z).astype(bf16)
    value = dot(choose, marks_col, ((1,), (1,))).astype(i32)
    q = lax.broadcasted_iota(i32, (block, col), 0)
    t = lax.broadcasted_iota(i32, (block, col), 1)
    wanted = jnp.where(q // cap == t // tok_dev, q % cap + 1, -1)
    pick = (value[:, None, :] == wanted[None, :, :]).astype(bf16).reshape(rows, col)

    xs = []
    for c in range(CHUNKS):
        sent = dot(pick, gathered[c][:, :part]).astype(bf16)
        got = exchange_plane(sent.reshape(lanes_of_plane, block, part))
        xs.append(got.reshape(rows, part))
    pre = dot(xs[0], full_w[:part])
    for c in range(1, CHUNKS):
        pre = pre + dot(xs[c], full_w[c * part : (c + 1) * part])
    sig = jax.nn.sigmoid(pre)
    grad_pre = (rows_g.astype(f32) * sig * (1.0 + pre * (1.0 - sig))).astype(bf16)

    grads = []
    for c in range(CHUNKS):
        back = dot(grad_pre, full_w[c * part : (c + 1) * part], ((1,), (1,))).astype(bf16)
        back = exchange_plane(back.reshape(lanes_of_plane, block, part))
        summed = dot(pick, back.reshape(rows, part), ((0,), (0,))).astype(bf16)
        grads.append(lax.psum_scatter(summed, "z", scatter_dimension=0, tiled=True))
    token_grad = jnp.concatenate(grads, axis=1)

    dw = jnp.concatenate([dot(x, grad_pre, ((0,), (0,))).astype(bf16) for x in xs], axis=0)
    dw = dw.reshape(2, 2, shard, hidden)
    to_core = lax.dynamic_slice_in_dim(dw, 1 - core, 1, axis=1)[:, 0]
    kept = lax.dynamic_slice_in_dim(dw, core, 1, axis=1)[:, 0]
    both = kept.astype(f32) + swapped(to_core, "core").astype(f32)
    mine = lax.dynamic_slice_in_dim(both, xl, 1, axis=0)[0]
    other = lax.dynamic_slice_in_dim(both, 1 - xl, 1, axis=0)[0].astype(bf16)
    moving = jnp.sum(jnp.where(jnp.arange(slots, dtype=i32) == here, swap_mask, 0)) == 1
    size = shard // SWAP_PARTS
    steps = []
    for s in range(SWAP_PARTS):
        at = slice(s * size, (s + 1) * size)
        grad = mine[at] + swapped(other[at], "xl").astype(f32)
        step = adam_direction(grad, first_moment[0, at], second_moment[0, at])
        steps.append(jnp.where(moving, swapped(step, "xh"), step))
    adam_step = jnp.concatenate(steps, axis=0)[None]
    return (token_grad, adam_step)


def solution(mesh):
    names = ("xl", "core", "xh", "y", "z")
    fine = Mesh(mesh.devices.reshape(2, 2, 2, 4, 8), names)
    dp, expert = ("xl", "core"), ("xh", "y", "z")
    in_specs = (
        P(names, None),
        P(names, None),
        P(names, None, None),
        P(),
        P(),
        P(expert, dp, None),
        P(expert, dp, None),
        P(expert, dp, None),
    )
    out_specs = (P(names, None), P(expert, dp, None))
    return jax.shard_map(step, mesh=fine, in_specs=in_specs, out_specs=out_specs, check_vma=False)
```

```python
import functools

import jax
import jax.numpy as jnp
import numpy as np
from jax import lax
from jax.experimental import pallas as pl
from jax.experimental.pallas import tpu as pltpu
from jax.sharding import Mesh, PartitionSpec as P

CAP = 12
PLANES = 8
LANES = 8
GROUPS = ((-1, 1), (-2, 2), (0, -4), (-3, 3))
BACK = (2, 3, 1, 0)
SWAP_PARTS = 2


def adam_direction(grad, first, second):
    first_new = 0.9 * first + 0.1 * grad
    second_new = 0.95 * second + 0.05 * grad * grad
    return (first_new / (jnp.sqrt(second_new) + 1e-08)).astype(jnp.bfloat16)


def dot(a, b, contract=((1,), (0,))):
    return lax.dot_general(a, b, (contract, ((), ())), preferred_element_type=jnp.float32)


def flipped_groups(with_z):
    nz = PLANES if with_z else 1
    return [
        [
            (((low ^ high) * 2 + high) * 4 + y) * nz + z
            for high in range(2)
            for y in range(4)
            for z in range(nz)
        ]
        for low in range(2)
    ]


def exchange_plane(block):
    return lax.all_to_all(
        block, ("xl", "xh", "y"), 0, 0, axis_index_groups=flipped_groups(False), tiled=True
    )


def exchange_all(block):
    return lax.all_to_all(
        block, ("xl", "xh", "y", "z"), 0, 0, axis_index_groups=flipped_groups(True), tiled=True
    )


def swapped(block, axis):
    return lax.ppermute(block, axis, [(0, 1), (1, 0)])


def shifted(block, by):
    return lax.ppermute(block, "z", [(i, (i + by) % PLANES) for i in range(PLANES)])


def dw_kernel(count, me, *refs):
    xs, g, out, joined = refs[:count], refs[count], refs[count + 1], refs[count + 2]
    rows = xs[0].shape[0]
    for i, x in enumerate(xs):
        joined[pl.ds(i * rows, rows), :] = x[...]
    out[0] = dot(joined[...], g[...], ((0,), (0,))).astype(out.dtype)


def weight_grad(me, xs, g, odd):
    rows, width = xs[0].shape
    hidden = g.shape[1]
    shard = width // 4
    bn = 512
    per = shard // bn
    spec = pl.BlockSpec((rows, bn), lambda h, i, m: (0, jnp.bitwise_xor(2 * h + odd, m[0]) * per + i))
    return pl.pallas_call(
        functools.partial(dw_kernel, len(xs)),
        grid_spec=pltpu.PrefetchScalarGridSpec(
            num_scalar_prefetch=1,
            grid=(2, per),
            in_specs=[spec] * len(xs) + [pl.BlockSpec(g.shape, lambda h, i, m: (0, 0))],
            out_specs=pl.BlockSpec((1, bn, hidden), lambda h, i, m: (h, i, 0)),
            scratch_shapes=[pltpu.VMEM((rows * len(xs), bn), jnp.bfloat16)],
        ),
        out_shape=jax.ShapeDtypeStruct((2, shard, hidden), jnp.bfloat16),
        cost_estimate=pl.CostEstimate(
            flops=2 * rows * len(xs) * width // 2 * hidden,
            bytes_accessed=rows * len(xs) * width + width * hidden + g.size * 2,
            transcendentals=0,
        ),
    )(me, *xs, g)


def step(
    tokens, token_experts, hidden_grad, held_expert, swap_mask, weight, first_moment, second_moment
):
    bf16, f32, i32 = jnp.bfloat16, jnp.float32, jnp.int32
    xl, core, xh = lax.axis_index("xl"), lax.axis_index("core"), lax.axis_index("xh")
    y, z = lax.axis_index("y"), lax.axis_index("z")
    here = (xh * 4 + y) * PLANES + z
    me = xl * 2 + core
    tok_dev, top = token_experts.shape
    width, hidden = tokens.shape[1], hidden_grad.shape[2]
    slots = held_expert.shape[0]
    pair = 2 * CAP
    group_rows = LANES * pair

    w_own = weight[0]
    w_x = swapped(w_own, "xl")
    w_c = swapped(w_own, "core")
    w_xc = swapped(w_x, "core")
    shard = w_own.shape[0]
    full_w = jnp.zeros((width, hidden), bf16)
    for piece, at in ((w_own, me), (w_c, me ^ 1), (w_x, me ^ 2), (w_xc, me ^ 3)):
        full_w = lax.dynamic_update_slice(full_w, piece, (at * shard, 0))

    same = token_experts[:, :, None] == held_expert[None, None, :]
    named = jnp.sum(same.astype(f32), axis=1).astype(bf16)
    earlier = jnp.asarray(np.tril(np.ones((tok_dev, tok_dev)), -1), bf16)
    rank = named.astype(f32) * (dot(earlier, named) + 1.0)

    marks = jnp.pad(rank.astype(bf16), ((0, 0), (0, 128 - slots)))
    own = jnp.concatenate([tokens, marks], axis=1)
    column = {0: own}
    for k in range(1, 5):
        column[-k] = shifted(column[1 - k], 1)
        if k < 4:
            column[k] = shifted(column[k - 1], -1)

    place = jnp.asarray(np.arange(slots) * CAP - 1.0, f32)
    slot = jnp.sum(jnp.where(same, (rank + place[None, :])[:, None, :], 0.0), axis=2)
    slot = slot.astype(i32).reshape(1, tok_dev * top)
    pick_g = (lax.broadcasted_iota(i32, (slots * CAP, tok_dev * top), 0) == slot).astype(bf16)
    send_g = dot(pick_g, hidden_grad.reshape(tok_dev * top, hidden)).astype(bf16)
    got_g = exchange_all(send_g.reshape(slots, CAP, hidden))
    got_g = got_g.reshape(slots * CAP, hidden)
    order = [(c, s, r) for two in GROUPS for c in range(LANES) for s in two for r in range(CAP)]
    base = np.array([c * PLANES * CAP + r for c, s, r in order], np.int32)[:, None]
    away = np.array([s % PLANES for c, s, r in order], np.int32)[:, None]
    source = jnp.asarray(base) + jnp.bitwise_and(jnp.asarray(away) + z, PLANES - 1) * CAP
    reorder = (source == lax.broadcasted_iota(i32, (slots * CAP, slots * CAP), 1)).astype(bf16)
    rows_g = dot(reorder, got_g).astype(bf16)

    def exchange(sent):
        got = exchange_plane(sent.reshape(LANES, pair, width))
        return got.reshape(group_rows, width)

    lane_i = lax.broadcasted_iota(i32, (LANES, slots), 0)
    slot_i = lax.broadcasted_iota(i32, (LANES, slots), 1)
    choose = (slot_i == lane_i * PLANES + z).astype(bf16)
    q, t = np.arange(pair)[:, None], np.arange(2 * tok_dev)[None, :]
    wanted = jnp.asarray(np.where(q // CAP == t // tok_dev, q % CAP + 1.0, -1.0)[None], f32)

    picks, xs, grads = [], [], []
    sent = None
    for n, (a, b) in enumerate(GROUPS):
        two = (column[a], column[b])
        if n > 0:
            *two, sent = lax.optimization_barrier((*two, sent))
            got = exchange(sent)
            xs.append(got)
        both = jnp.concatenate(two, axis=0)
        value = dot(choose, both[:, width : width + slots], ((1,), (1,)))
        pick = (value[:, None, :] == wanted).astype(bf16).reshape(group_rows, 2 * tok_dev)
        sent = dot(pick, both[:, :width]).astype(bf16)
        picks.append(pick)
    xs.append(exchange(sent))
    for n in range(len(GROUPS)):
        if n > 0:
            xs[n], _ = lax.optimization_barrier((xs[n], grads[n - 1]))
        pre = dot(xs[n], full_w)
        sig = jax.nn.sigmoid(pre)
        g = rows_g[n * group_rows : (n + 1) * group_rows].astype(f32)
        g = (g * sig * (1.0 + pre * (1.0 - sig))).astype(bf16)
        grads.append(lax.optimization_barrier(g))

    going = {}
    for n in BACK:
        back = dot(grads[n], full_w, ((1,), (1,))).astype(bf16)
        back = exchange_plane(back.reshape(LANES, pair, width))
        back = back.reshape(group_rows, width)
        for i, s in enumerate(GROUPS[n]):
            part = dot(picks[n][:, i * tok_dev : (i + 1) * tok_dev], back, ((0,), (0,)))
            if s == 0:
                home = part
                continue
            sign = 1 if s > 0 else -1
            if sign in going:
                part = part + going[sign].astype(f32)
            going[sign] = shifted(part.astype(bf16), sign)
    token_grad = (home + going[1].astype(f32) + going[-1].astype(f32)).astype(bf16)

    grad_rows = jnp.concatenate(grads, axis=0)
    me_ref = me.astype(i32).reshape(1)
    to_core = weight_grad(me_ref, xs, grad_rows, 1)
    from_core = swapped(to_core, "core")
    kept = weight_grad(me_ref, xs, grad_rows, 0)
    other = (kept[1].astype(f32) + from_core[1].astype(f32)).astype(bf16)
    moving = jnp.sum(jnp.where(jnp.arange(slots, dtype=i32) == here, swap_mask, 0)) == 1
    size = shard // SWAP_PARTS
    steps = []
    for s in range(SWAP_PARTS):
        at = slice(s * size, (s + 1) * size)
        from_x = swapped(other[at], "xl")
        grad = kept[0, at].astype(f32) + from_core[0, at].astype(f32) + from_x.astype(f32)
        stepped = adam_direction(grad, first_moment[0, at], second_moment[0, at])
        partner = swapped(stepped, "xh")
        steps.append(jnp.where(moving, partner, stepped))
    adam_step = jnp.concatenate(steps, axis=0)[None]
    return (token_grad, adam_step)


def solution(mesh):
    names = ("xl", "core", "xh", "y", "z")
    fine = Mesh(mesh.devices.reshape(2, 2, 2, 4, 8), names)
    dp, expert = ("xl", "core"), ("xh", "y", "z")
    in_specs = (
        P(names, None),
        P(names, None),
        P(names, None, None),
        P(),
        P(),
        P(expert, dp, None),
        P(expert, dp, None),
        P(expert, dp, None),
    )
    out_specs = (P(names, None), P(expert, dp, None))
    return jax.shard_map(step, mesh=fine, in_specs=in_specs, out_specs=out_specs, check_vma=False)
```

```python
import functools

import jax
import jax.numpy as jnp
import numpy as np
from jax import lax
from jax.experimental import pallas as pl
from jax.experimental.pallas import tpu as pltpu
from jax.sharding import Mesh, PartitionSpec as P

CAP = 12
PLANES = 8
LANES = 8
GROUPS = ((-1, 1), (-2, 2), (0, -4), (-3, 3))
BACK = (2, 3, 1, 0)
SWAP_PARTS = 2


def adam_direction(grad, first, second):
    first_new = 0.9 * first + 0.1 * grad
    second_new = 0.95 * second + 0.05 * grad * grad
    return (first_new / (jnp.sqrt(second_new) + 1e-08)).astype(jnp.bfloat16)


def dot(a, b, contract=((1,), (0,))):
    return lax.dot_general(a, b, (contract, ((), ())), preferred_element_type=jnp.float32)


def flipped_groups(with_z):
    nz = PLANES if with_z else 1
    return [
        [
            (((low ^ high) * 2 + high) * 4 + y) * nz + z
            for high in range(2)
            for y in range(4)
            for z in range(nz)
        ]
        for low in range(2)
    ]


def exchange_plane(block):
    return lax.all_to_all(
        block, ("xl", "xh", "y"), 0, 0, axis_index_groups=flipped_groups(False), tiled=True
    )


def exchange_all(block):
    return lax.all_to_all(
        block, ("xl", "xh", "y", "z"), 0, 0, axis_index_groups=flipped_groups(True), tiled=True
    )


def swapped(block, axis):
    return lax.ppermute(block, axis, [(0, 1), (1, 0)])


def shifted(block, by):
    return lax.ppermute(block, "z", [(i, (i + by) % PLANES) for i in range(PLANES)])


def dw_kernel(count, me, *refs):
    xs, g, out, joined = refs[:count], refs[count], refs[count + 1], refs[count + 2]
    rows = xs[0].shape[0]
    for i, x in enumerate(xs):
        joined[pl.ds(i * rows, rows), :] = x[...]
    out[0] = dot(joined[...], g[...], ((0,), (0,))).astype(out.dtype)


def weight_grad(me, xs, g, odd):
    rows, width = xs[0].shape
    hidden = g.shape[1]
    shard = width // 4
    bn = 512
    per = shard // bn
    spec = pl.BlockSpec((rows, bn), lambda h, i, m: (0, jnp.bitwise_xor(2 * h + odd, m[0]) * per + i))
    return pl.pallas_call(
        functools.partial(dw_kernel, len(xs)),
        grid_spec=pltpu.PrefetchScalarGridSpec(
            num_scalar_prefetch=1,
            grid=(2, per),
            in_specs=[spec] * len(xs) + [pl.BlockSpec(g.shape, lambda h, i, m: (0, 0))],
            out_specs=pl.BlockSpec((1, bn, hidden), lambda h, i, m: (h, i, 0)),
            scratch_shapes=[pltpu.VMEM((rows * len(xs), bn), jnp.bfloat16)],
        ),
        out_shape=jax.ShapeDtypeStruct((2, shard, hidden), jnp.bfloat16),
        cost_estimate=pl.CostEstimate(
            flops=2 * rows * len(xs) * width // 2 * hidden,
            bytes_accessed=rows * len(xs) * width + width * hidden + g.size * 2,
            transcendentals=0,
        ),
    )(me, *xs, g)


def step(
    tokens, token_experts, hidden_grad, held_expert, swap_mask, weight, first_moment, second_moment
):
    bf16, f32, i32 = jnp.bfloat16, jnp.float32, jnp.int32
    xl, core, xh = lax.axis_index("xl"), lax.axis_index("core"), lax.axis_index("xh")
    y, z = lax.axis_index("y"), lax.axis_index("z")
    here = (xh * 4 + y) * PLANES + z
    me = xl * 2 + core
    tok_dev, top = token_experts.shape
    width, hidden = tokens.shape[1], hidden_grad.shape[2]
    slots = held_expert.shape[0]
    pair = 2 * CAP
    group_rows = LANES * pair

    w_own = weight[0]
    w_x = swapped(w_own, "xl")
    w_c = swapped(w_own, "core")
    w_xc = swapped(w_x, "core")
    shard = w_own.shape[0]
    full_w = jnp.zeros((width, hidden), bf16)
    for piece, at in ((w_own, me), (w_c, me ^ 1), (w_x, me ^ 2), (w_xc, me ^ 3)):
        full_w = lax.dynamic_update_slice(full_w, piece, (at * shard, 0))

    same = token_experts[:, :, None] == held_expert[None, None, :]
    named = jnp.sum(same.astype(f32), axis=1).astype(bf16)
    earlier = jnp.asarray(np.tril(np.ones((tok_dev, tok_dev)), -1), bf16)
    rank = named.astype(f32) * (dot(earlier, named) + 1.0)

    marks = jnp.pad(rank.astype(bf16), ((0, 0), (0, 128 - slots)))
    own = jnp.concatenate([tokens, marks], axis=1)
    column = {0: own}
    for k in range(1, 5):
        column[-k] = shifted(column[1 - k], 1)
        if k < 4:
            column[k] = shifted(column[k - 1], -1)

    place = jnp.asarray(np.arange(slots) * CAP - 1.0, f32)
    slot = jnp.sum(jnp.where(same, (rank + place[None, :])[:, None, :], 0.0), axis=2)
    slot = slot.astype(i32).reshape(1, tok_dev * top)
    pick_g = (lax.broadcasted_iota(i32, (slots * CAP, tok_dev * top), 0) == slot).astype(bf16)
    send_g = dot(pick_g, hidden_grad.reshape(tok_dev * top, hidden)).astype(bf16)
    got_g = exchange_all(send_g.reshape(slots, CAP, hidden))
    got_g = got_g.reshape(slots * CAP, hidden)
    order = [(c, s, r) for two in GROUPS for c in range(LANES) for s in two for r in range(CAP)]
    base = np.array([c * PLANES * CAP + r for c, s, r in order], np.int32)[:, None]
    away = np.array([s % PLANES for c, s, r in order], np.int32)[:, None]
    source = jnp.asarray(base) + jnp.bitwise_and(jnp.asarray(away) + z, PLANES - 1) * CAP
    reorder = (source == lax.broadcasted_iota(i32, (slots * CAP, slots * CAP), 1)).astype(bf16)
    rows_g = dot(reorder, got_g).astype(bf16)

    def exchange(sent):
        got = exchange_plane(sent.reshape(LANES, pair, width))
        return got.reshape(group_rows, width)

    lane_i = lax.broadcasted_iota(i32, (LANES, slots), 0)
    slot_i = lax.broadcasted_iota(i32, (LANES, slots), 1)
    choose = (slot_i == lane_i * PLANES + z).astype(bf16)
    q, t = np.arange(pair)[:, None], np.arange(2 * tok_dev)[None, :]
    wanted = jnp.asarray(np.where(q // CAP == t // tok_dev, q % CAP + 1.0, -1.0)[None], f32)

    picks, xs, grads = [], [], []
    sent = None
    for n, (a, b) in enumerate(GROUPS):
        two = (column[a], column[b])
        if n > 0:
            xs.append(exchange(sent))
            *two, _ = lax.optimization_barrier((*two, sent))
        both = jnp.concatenate(two, axis=0)
        value = dot(choose, both[:, width : width + slots], ((1,), (1,)))
        pick = (value[:, None, :] == wanted).astype(bf16).reshape(group_rows, 2 * tok_dev)
        sent = dot(pick, both[:, :width]).astype(bf16)
        picks.append(pick)
    xs.append(exchange(sent))
    for n in range(len(GROUPS)):
        if n > 0:
            xs[n], _ = lax.optimization_barrier((xs[n], grads[n - 1]))
        pre = dot(xs[n], full_w)
        sig = jax.nn.sigmoid(pre)
        g = rows_g[n * group_rows : (n + 1) * group_rows].astype(f32)
        g = (g * sig * (1.0 + pre * (1.0 - sig))).astype(bf16)
        grads.append(lax.optimization_barrier(g))

    going = {}
    for n in BACK:
        back = dot(grads[n], full_w, ((1,), (1,))).astype(bf16)
        back = exchange_plane(back.reshape(LANES, pair, width))
        back = back.reshape(group_rows, width)
        for i, s in enumerate(GROUPS[n]):
            sign = 1 if s > 0 else -1
            part = dot(picks[n][:, i * tok_dev : (i + 1) * tok_dev], back, ((0,), (0,)))
            if s == 0:
                home = part
                continue
            if sign in going:
                part = part + going[sign].astype(f32)
            going[sign] = shifted(part.astype(bf16), sign)
    token_grad = (home + going[1].astype(f32) + going[-1].astype(f32)).astype(bf16)

    grad_rows = jnp.concatenate(grads, axis=0)
    me_ref = me.astype(i32).reshape(1)
    to_core = weight_grad(me_ref, xs, grad_rows, 1)
    from_core = swapped(to_core, "core")
    kept = weight_grad(me_ref, xs, grad_rows, 0)
    other = (kept[1].astype(f32) + from_core[1].astype(f32)).astype(bf16)
    moving = jnp.sum(jnp.where(jnp.arange(slots, dtype=i32) == here, swap_mask, 0)) == 1
    size = shard // SWAP_PARTS
    steps = []
    for s in range(SWAP_PARTS):
        at = slice(s * size, (s + 1) * size)
        from_x = swapped(other[at], "xl")
        grad = kept[0, at].astype(f32) + from_core[0, at].astype(f32) + from_x.astype(f32)
        stepped = adam_direction(grad, first_moment[0, at], second_moment[0, at])
        partner = swapped(stepped, "xh")
        steps.append(jnp.where(moving, partner, stepped))
    adam_step = jnp.concatenate(steps, axis=0)[None]
    return (token_grad, adam_step)


def solution(mesh):
    names = ("xl", "core", "xh", "y", "z")
    fine = Mesh(mesh.devices.reshape(2, 2, 2, 4, 8), names)
    dp, expert = ("xl", "core"), ("xh", "y", "z")
    in_specs = (
        P(names, None),
        P(names, None),
        P(names, None, None),
        P(),
        P(),
        P(expert, dp, None),
        P(expert, dp, None),
        P(expert, dp, None),
    )
    out_specs = (P(names, None), P(expert, dp, None))
    return jax.shard_map(step, mesh=fine, in_specs=in_specs, out_specs=out_specs, check_vma=False)
```

```python
import functools

import jax
import jax.numpy as jnp
import numpy as np
from jax import lax
from jax.experimental import pallas as pl
from jax.experimental.pallas import tpu as pltpu
from jax.sharding import Mesh, PartitionSpec as P

CAP = 12
PLANES = 8
LANES = 8
GROUPS = ((-1, 1), (-2, 2), (0, -4), (-3, 3))
BACK = (2, 3, 1, 0)
SWAP_PARTS = 2


def adam_direction(grad, first, second):
    first_new = 0.9 * first + 0.1 * grad
    second_new = 0.95 * second + 0.05 * grad * grad
    return (first_new / (jnp.sqrt(second_new) + 1e-08)).astype(jnp.bfloat16)


def dot(a, b, contract=((1,), (0,))):
    return lax.dot_general(a, b, (contract, ((), ())), preferred_element_type=jnp.float32)


def exchange_plane(block):
    groups = [
        [((low ^ high) * 2 + high) * 4 + y for high in range(2) for y in range(4)]
        for low in range(2)
    ]
    return lax.all_to_all(block, ("xl", "xh", "y"), 0, 0, axis_index_groups=groups, tiled=True)


def swapped(block, axis):
    return lax.ppermute(block, axis, [(0, 1), (1, 0)])


def shifted(block, by):
    return lax.ppermute(block, "z", [(i, (i + by) % PLANES) for i in range(PLANES)])


def dw_kernel(count, me, *refs):
    xs, g, out, joined = refs[:count], refs[count], refs[count + 1], refs[count + 2]
    rows = xs[0].shape[0]
    for i, x in enumerate(xs):
        joined[pl.ds(i * rows, rows), :] = x[...]
    out[0] = dot(joined[...], g[...], ((0,), (0,))).astype(out.dtype)


def weight_grad(me, xs, g, odd):
    rows, hidden = xs[0].shape[0], g.shape[1]
    width = xs[0].shape[1] - hidden
    shard = width // 4
    bn = 512
    per = shard // bn
    spec = pl.BlockSpec((rows, bn), lambda h, i, m: (0, jnp.bitwise_xor(2 * h + odd, m[0]) * per + i))
    return pl.pallas_call(
        functools.partial(dw_kernel, len(xs)),
        grid_spec=pltpu.PrefetchScalarGridSpec(
            num_scalar_prefetch=1,
            grid=(2, per),
            in_specs=[spec] * len(xs) + [pl.BlockSpec(g.shape, lambda h, i, m: (0, 0))],
            out_specs=pl.BlockSpec((1, bn, hidden), lambda h, i, m: (h, i, 0)),
            scratch_shapes=[pltpu.VMEM((rows * len(xs), bn), jnp.bfloat16)],
        ),
        out_shape=jax.ShapeDtypeStruct((2, shard, hidden), jnp.bfloat16),
        cost_estimate=pl.CostEstimate(
            flops=2 * rows * len(xs) * width // 2 * hidden,
            bytes_accessed=rows * len(xs) * width + width * hidden + g.size * 2,
            transcendentals=0,
        ),
    )(me, *xs, g)


def pack_kernel(choose, wanted, perm, ca, cb, ga, gb, sent, pick, tokens, hidden):
    tok_dev, rows_g = ca.shape[0], ga.shape[0]
    width = sent.shape[1] - ga.shape[1]
    tokens[:tok_dev] = ca[...]
    tokens[tok_dev:] = cb[...]
    hidden[:rows_g] = ga[...]
    hidden[rows_g:] = gb[...]
    value = dot(choose[...], tokens[:, width:], ((1,), (1,)))
    hit = (value[:, None, :] == wanted[...][None]).astype(jnp.float32)
    chosen = hit.reshape(pick.shape).astype(jnp.bfloat16)
    pick[...] = chosen
    bn = 512

    def columns(i, carry):
        at = pl.ds(pl.multiple_of(i * bn, bn), bn)
        sent[:, at] = dot(chosen, tokens[:, at]).astype(sent.dtype)
        return carry

    lax.fori_loop(0, width // bn, columns, 0)
    sent[:, width:] = dot(perm[...], hidden[...]).astype(sent.dtype)


def pack(choose, wanted, perm, ca, cb, ga, gb, width):
    rows, hidden = perm.shape[0], ga.shape[1]
    return pl.pallas_call(
        pack_kernel,
        out_shape=(
            jax.ShapeDtypeStruct((rows, width + hidden), jnp.bfloat16),
            jax.ShapeDtypeStruct((rows, 2 * ca.shape[0]), jnp.bfloat16),
        ),
        scratch_shapes=[
            pltpu.VMEM((2 * ca.shape[0], ca.shape[1]), jnp.bfloat16),
            pltpu.VMEM((2 * ga.shape[0], hidden), jnp.bfloat16),
        ],
        name="pack",
    )(choose, wanted, perm, ca, cb, ga, gb)


def expert_kernel(steps, x, g0, g1, g2, w, back, grad, acc):
    phase, k = pl.program_id(0), pl.program_id(1)

    @pl.when(phase == 0)
    def _():
        part = dot(x[...], w[...])

        @pl.when(k == 0)
        def _():
            acc[...] = part

        @pl.when(k > 0)
        def _():
            acc[...] += part

        @pl.when(k == steps - 1)
        def _():
            wide = g0.shape[1]
            for i, g in enumerate((g0, g1, g2)):
                at = pl.ds(i * wide, wide)
                pre = acc[:, at]
                sig = jax.nn.sigmoid(pre)
                value = g[...].astype(jnp.float32) * sig * (1.0 + pre * (1.0 - sig))
                grad[:, at] = value.astype(grad.dtype)

    @pl.when(phase == 1)
    def _():
        back[...] = dot(grad[...], w[...], ((1,), (1,))).astype(back.dtype)


def expert(got, full_w):
    width, hidden = full_w.shape
    rows = got.shape[0]
    kb = 512
    nk = width // kb
    third = hidden // 3
    side = [pl.BlockSpec((rows, third), lambda p, k, i=i: (0, width // third + i)) for i in range(3)]
    return pl.pallas_call(
        functools.partial(expert_kernel, nk),
        grid=(2, nk),
        in_specs=[pl.BlockSpec((rows, kb), lambda p, k: (0, jnp.where(p == 0, k, nk - 1)))]
        + side
        + [pl.BlockSpec((kb, hidden), lambda p, k: (k, 0))],
        out_specs=(
            pl.BlockSpec((rows, kb), lambda p, k: (0, jnp.where(p == 0, 0, k))),
            pl.BlockSpec((rows, hidden), lambda p, k: (0, 0)),
        ),
        out_shape=(
            jax.ShapeDtypeStruct((rows, width), jnp.bfloat16),
            jax.ShapeDtypeStruct((rows, hidden), jnp.bfloat16),
        ),
        scratch_shapes=[pltpu.VMEM((rows, hidden), jnp.float32)],
        cost_estimate=pl.CostEstimate(
            flops=4 * rows * width * hidden,
            bytes_accessed=4 * width * (hidden + rows),
            transcendentals=rows * hidden,
        ),
        name="expert",
    )(got, got, got, got, full_w)


def step(
    tokens, token_experts, hidden_grad, held_expert, swap_mask, weight, first_moment, second_moment
):
    bf16, f32, i32 = jnp.bfloat16, jnp.float32, jnp.int32
    xl, core, xh = lax.axis_index("xl"), lax.axis_index("core"), lax.axis_index("xh")
    y, z = lax.axis_index("y"), lax.axis_index("z")
    here = (xh * 4 + y) * PLANES + z
    me = xl * 2 + core
    tok_dev, top = token_experts.shape
    width, hidden = tokens.shape[1], hidden_grad.shape[2]
    slots = held_expert.shape[0]
    pair = 2 * CAP
    group_rows = LANES * pair

    w_own = weight[0]
    w_x = swapped(w_own, "xl")
    w_c = swapped(w_own, "core")
    w_xc = swapped(w_x, "core")
    shard = w_own.shape[0]
    full_w = jnp.zeros((width, hidden), bf16)
    for piece, at in ((w_own, me), (w_c, me ^ 1), (w_x, me ^ 2), (w_xc, me ^ 3)):
        full_w = lax.dynamic_update_slice(full_w, piece, (at * shard, 0))

    same = token_experts[:, :, None] == held_expert[None, None, :]
    named = jnp.sum(same.astype(f32), axis=1).astype(bf16)
    earlier = jnp.asarray(np.tril(np.ones((tok_dev, tok_dev)), -1), bf16)
    rank = named.astype(f32) * (dot(earlier, named) + 1.0)

    marks = jnp.pad(rank.astype(bf16), ((0, 0), (0, 128 - slots)))
    own = jnp.concatenate([tokens, marks], axis=1)
    column = {0: own}
    for k in range(1, 5):
        column[-k] = shifted(column[1 - k], 1)
        if k < 4:
            column[k] = shifted(column[k - 1], -1)

    slot_p = np.arange(slots)
    ahead = jnp.bitwise_and(jnp.asarray(slot_p % PLANES, i32) - z, PLANES - 1) * (LANES * CAP)
    place = (ahead + jnp.asarray(slot_p // PLANES * CAP - 1, i32)).astype(f32)
    slot = jnp.sum(jnp.where(same, (rank + place[None, :])[:, None, :], 0.0), axis=2)
    slot = slot.astype(i32).reshape(1, tok_dev * top)
    pick_g = (lax.broadcasted_iota(i32, (slots * CAP, tok_dev * top), 0) == slot).astype(bf16)
    send_g = dot(pick_g, hidden_grad.reshape(tok_dev * top, hidden)).astype(bf16)
    send_g = send_g.reshape(PLANES, LANES * CAP, hidden)
    grad_from = {0: send_g[0]}
    for d in (1, -1, 2, -2, 4, 3, -3):
        grad_from[-d] = shifted(send_g[d % PLANES], d)

    lane_i = lax.broadcasted_iota(i32, (LANES, 128), 0)
    slot_i = lax.broadcasted_iota(i32, (LANES, 128), 1)
    choose = (slot_i == lane_i * PLANES + z).astype(bf16)
    q, t = np.arange(pair)[:, None], np.arange(2 * tok_dev)[None, :]
    wanted = jnp.asarray(np.where(q // CAP == t // tok_dev, q % CAP + 1.0, -1.0), f32)
    order = [(s * LANES + j) * CAP + r for j in range(LANES) for s in range(2) for r in range(CAP)]
    perm = jnp.asarray(np.arange(group_rows)[None, :] == np.array(order)[:, None], bf16)

    picks, xs, grads, backs = [], [], [], []
    for a, b in GROUPS:
        sent, pick = pack(
            choose, wanted, perm, column[a], column[b], grad_from[a], grad_from[b], width
        )
        got = exchange_plane(sent.reshape(LANES, pair, width + hidden))
        got = got.reshape(group_rows, width + hidden)
        back, grad = expert(got, full_w)
        picks.append(pick)
        xs.append(got)
        grads.append(grad)
        backs.append(back)

    going = {}
    for n in BACK:
        back = exchange_plane(backs[n].reshape(LANES, pair, width))
        back = back.reshape(group_rows, width)
        for i, s in enumerate(GROUPS[n]):
            sign = 1 if s > 0 else -1
            part = dot(picks[n][:, i * tok_dev : (i + 1) * tok_dev], back, ((0,), (0,)))
            if s == 0:
                home = part
                continue
            if sign in going:
                part = part + going[sign].astype(f32)
            going[sign] = shifted(part.astype(bf16), sign)
    token_grad = (home + going[1].astype(f32) + going[-1].astype(f32)).astype(bf16)

    grad_rows = jnp.concatenate(grads, axis=0)
    me_ref = me.astype(i32).reshape(1)
    to_core = weight_grad(me_ref, xs, grad_rows, 1)
    from_core = swapped(to_core, "core")
    kept = weight_grad(me_ref, xs, grad_rows, 0)
    other = (kept[1].astype(f32) + from_core[1].astype(f32)).astype(bf16)
    moving = jnp.sum(jnp.where(jnp.arange(slots, dtype=i32) == here, swap_mask, 0)) == 1
    size = shard // SWAP_PARTS
    steps = []
    for s in range(SWAP_PARTS):
        at = slice(s * size, (s + 1) * size)
        from_x = swapped(other[at], "xl")
        if s > 0:
            from_x, _ = lax.optimization_barrier((from_x, stepped))
        grad = kept[0, at].astype(f32) + from_core[0, at].astype(f32) + from_x.astype(f32)
        stepped = adam_direction(grad, first_moment[0, at], second_moment[0, at])
        partner = swapped(stepped, "xh")
        steps.append(jnp.where(moving, partner, stepped))
    adam_step = jnp.concatenate(steps, axis=0)[None]
    return (token_grad, adam_step)


def solution(mesh):
    names = ("xl", "core", "xh", "y", "z")
    fine = Mesh(mesh.devices.reshape(2, 2, 2, 4, 8), names)
    dp, expert = ("xl", "core"), ("xh", "y", "z")
    in_specs = (
        P(names, None),
        P(names, None),
        P(names, None, None),
        P(),
        P(),
        P(expert, dp, None),
        P(expert, dp, None),
        P(expert, dp, None),
    )
    out_specs = (P(names, None), P(expert, dp, None))
    return jax.shard_map(step, mesh=fine, in_specs=in_specs, out_specs=out_specs, check_vma=False)
```

```python
import functools

import jax
import jax.numpy as jnp
import numpy as np
from jax import lax
from jax.experimental import pallas as pl
from jax.experimental.pallas import tpu as pltpu
from jax.sharding import Mesh, PartitionSpec as P

CAP = 12
PLANES = 8
LANES = 8
GROUPS = ((-1, 1), (-2, 2), (0, -4), (-3, 3))
BACK = (2, 3, 1, 0)
SWAP_PARTS = 2


def adam_direction(grad, first, second):
    first_new = 0.9 * first + 0.1 * grad
    second_new = 0.95 * second + 0.05 * grad * grad
    return (first_new / (jnp.sqrt(second_new) + 1e-08)).astype(jnp.bfloat16)


def dot(a, b, contract=((1,), (0,))):
    return lax.dot_general(a, b, (contract, ((), ())), preferred_element_type=jnp.float32)


def exchange_plane(block):
    groups = [
        [((low ^ high) * 2 + high) * 4 + y for high in range(2) for y in range(4)]
        for low in range(2)
    ]
    return lax.all_to_all(block, ("xl", "xh", "y"), 0, 0, axis_index_groups=groups, tiled=True)


def swapped(block, axis):
    return lax.ppermute(block, axis, [(0, 1), (1, 0)])


def shifted(block, by):
    return lax.ppermute(block, "z", [(i, (i + by) % PLANES) for i in range(PLANES)])


def dw_kernel(count, me, *refs):
    xs, g, out, joined = refs[:count], refs[count], refs[count + 1], refs[count + 2]
    rows = xs[0].shape[0]
    for i, x in enumerate(xs):
        joined[pl.ds(i * rows, rows), :] = x[...]
    out[0] = dot(joined[...], g[...], ((0,), (0,))).astype(out.dtype)


def weight_grad(me, xs, g, odd):
    rows, hidden = xs[0].shape[0], g.shape[1]
    width = xs[0].shape[1] - hidden
    shard = width // 4
    bn = 512
    per = shard // bn
    spec = pl.BlockSpec((rows, bn), lambda h, i, m: (0, jnp.bitwise_xor(2 * h + odd, m[0]) * per + i))
    return pl.pallas_call(
        functools.partial(dw_kernel, len(xs)),
        grid_spec=pltpu.PrefetchScalarGridSpec(
            num_scalar_prefetch=1,
            grid=(2, per),
            in_specs=[spec] * len(xs) + [pl.BlockSpec(g.shape, lambda h, i, m: (0, 0))],
            out_specs=pl.BlockSpec((1, bn, hidden), lambda h, i, m: (h, i, 0)),
            scratch_shapes=[pltpu.VMEM((rows * len(xs), bn), jnp.bfloat16)],
        ),
        out_shape=jax.ShapeDtypeStruct((2, shard, hidden), jnp.bfloat16),
        cost_estimate=pl.CostEstimate(
            flops=2 * rows * len(xs) * width // 2 * hidden,
            bytes_accessed=rows * len(xs) * width + width * hidden + g.size * 2,
            transcendentals=0,
        ),
    )(me, *xs, g)


def pack_kernel(choose, wanted, perm, ca, cb, ga, gb, sent, pick, tokens, hidden):
    tok_dev, rows_g = ca.shape[0], ga.shape[0]
    width = sent.shape[1] - ga.shape[1]
    tokens[:tok_dev] = ca[...]
    tokens[tok_dev:] = cb[...]
    hidden[:rows_g] = ga[...]
    hidden[rows_g:] = gb[...]
    value = dot(choose[...], tokens[:, width:], ((1,), (1,)))
    hit = (value[:, None, :] == wanted[...][None]).astype(jnp.float32)
    chosen = hit.reshape(pick.shape).astype(jnp.bfloat16)
    pick[...] = chosen
    bn = 512

    def columns(i, carry):
        at = pl.ds(pl.multiple_of(i * bn, bn), bn)
        sent[:, at] = dot(chosen, tokens[:, at]).astype(sent.dtype)
        return carry

    lax.fori_loop(0, width // bn, columns, 0)
    sent[:, width:] = dot(perm[...], hidden[...]).astype(sent.dtype)


def pack(choose, wanted, perm, ca, cb, ga, gb, width):
    rows, hidden = perm.shape[0], ga.shape[1]
    return pl.pallas_call(
        pack_kernel,
        out_shape=(
            jax.ShapeDtypeStruct((rows, width + hidden), jnp.bfloat16),
            jax.ShapeDtypeStruct((rows, 2 * ca.shape[0]), jnp.bfloat16),
        ),
        scratch_shapes=[
            pltpu.VMEM((2 * ca.shape[0], ca.shape[1]), jnp.bfloat16),
            pltpu.VMEM((2 * ga.shape[0], hidden), jnp.bfloat16),
        ],
        name="pack",
    )(choose, wanted, perm, ca, cb, ga, gb)


def expert_kernel(steps, x, g0, g1, g2, w, back, grad, acc):
    phase, k = pl.program_id(0), pl.program_id(1)

    @pl.when(phase == 0)
    def _():
        part = dot(x[...], w[...])

        @pl.when(k == 0)
        def _():
            acc[...] = part

        @pl.when(k > 0)
        def _():
            acc[...] += part

        @pl.when(k == steps - 1)
        def _():
            wide = g0.shape[1]
            for i, g in enumerate((g0, g1, g2)):
                at = pl.ds(i * wide, wide)
                pre = acc[:, at]
                sig = jax.nn.sigmoid(pre)
                value = g[...].astype(jnp.float32) * sig * (1.0 + pre * (1.0 - sig))
                grad[:, at] = value.astype(grad.dtype)

    @pl.when(phase == 1)
    def _():
        back[...] = dot(grad[...], w[...], ((1,), (1,))).astype(back.dtype)


def expert(got, full_w):
    width, hidden = full_w.shape
    rows = got.shape[0]
    kb = 1024
    nk = width // kb
    third = hidden // 3
    side = [pl.BlockSpec((rows, third), lambda p, k, i=i: (0, width // third + i)) for i in range(3)]
    return pl.pallas_call(
        functools.partial(expert_kernel, nk),
        grid=(2, nk),
        in_specs=[pl.BlockSpec((rows, kb), lambda p, k: (0, jnp.where(p == 0, k, nk - 1)))]
        + side
        + [pl.BlockSpec((kb, hidden), lambda p, k: (k, 0))],
        out_specs=(
            pl.BlockSpec((rows, kb), lambda p, k: (0, jnp.where(p == 0, 0, k))),
            pl.BlockSpec((rows, hidden), lambda p, k: (0, 0)),
        ),
        out_shape=(
            jax.ShapeDtypeStruct((rows, width), jnp.bfloat16),
            jax.ShapeDtypeStruct((rows, hidden), jnp.bfloat16),
        ),
        scratch_shapes=[pltpu.VMEM((rows, hidden), jnp.float32)],
        cost_estimate=pl.CostEstimate(
            flops=4 * rows * width * hidden,
            bytes_accessed=4 * width * (hidden + rows),
            transcendentals=rows * hidden,
        ),
        name="expert",
    )(got, got, got, got, full_w)


def step(
    tokens, token_experts, hidden_grad, held_expert, swap_mask, weight, first_moment, second_moment
):
    bf16, f32, i32 = jnp.bfloat16, jnp.float32, jnp.int32
    xl, core, xh = lax.axis_index("xl"), lax.axis_index("core"), lax.axis_index("xh")
    y, z = lax.axis_index("y"), lax.axis_index("z")
    here = (xh * 4 + y) * PLANES + z
    me = xl * 2 + core
    tok_dev, top = token_experts.shape
    width, hidden = tokens.shape[1], hidden_grad.shape[2]
    slots = held_expert.shape[0]
    pair = 2 * CAP
    group_rows = LANES * pair

    w_own = weight[0]
    w_x = swapped(w_own, "xl")
    w_c = swapped(w_own, "core")
    w_xc = swapped(w_x, "core")
    shard = w_own.shape[0]
    full_w = jnp.zeros((width, hidden), bf16)
    for i, piece in enumerate((w_own, w_c, w_x, w_xc)):
        full_w = lax.dynamic_update_slice(full_w, piece, ((me ^ i) * shard, 0))

    same = token_experts[:, :, None] == held_expert[None, None, :]
    named = jnp.sum(same.astype(f32), axis=1).astype(bf16)
    earlier = jnp.asarray(np.tril(np.ones((tok_dev, tok_dev)), -1), bf16)
    rank = named.astype(f32) * (dot(earlier, named) + 1.0)

    marks = jnp.pad(rank.astype(bf16), ((0, 0), (0, 128 - slots)))
    own = jnp.concatenate([tokens, marks], axis=1)
    column = {0: own}
    for k in range(1, 5):
        column[-k] = shifted(column[1 - k], 1)
        if k < 4:
            column[k] = shifted(column[k - 1], -1)

    slot_p = np.arange(slots)
    ahead = jnp.bitwise_and(jnp.asarray(slot_p % PLANES, i32) - z, PLANES - 1) * (LANES * CAP)
    place = (ahead + jnp.asarray(slot_p // PLANES * CAP - 1, i32)).astype(f32)
    slot = jnp.sum(jnp.where(same, (rank + place[None, :])[:, None, :], 0.0), axis=2)
    slot = slot.astype(i32).reshape(1, tok_dev * top)
    pick_g = (lax.broadcasted_iota(i32, (slots * CAP, tok_dev * top), 0) == slot).astype(bf16)
    send_g = dot(pick_g, hidden_grad.reshape(tok_dev * top, hidden)).astype(bf16)
    send_g = send_g.reshape(PLANES, LANES * CAP, hidden)
    grad_from = {0: send_g[0]}
    for d in (1, -1, 2, -2, 4, 3, -3):
        grad_from[-d] = shifted(send_g[d % PLANES], d)

    lane_i = lax.broadcasted_iota(i32, (LANES, 128), 0)
    slot_i = lax.broadcasted_iota(i32, (LANES, 128), 1)
    choose = (slot_i == lane_i * PLANES + z).astype(bf16)
    q, t = np.arange(pair)[:, None], np.arange(2 * tok_dev)[None, :]
    wanted = jnp.asarray(np.where(q // CAP == t // tok_dev, q % CAP + 1.0, -1.0), f32)
    order = [(s * LANES + j) * CAP + r for j in range(LANES) for s in range(2) for r in range(CAP)]
    perm = jnp.asarray(np.arange(group_rows)[None, :] == np.array(order)[:, None], bf16)

    picks, xs, grads, backs = [], [], [], []
    for a, b in GROUPS:
        sent, pick = pack(
            choose, wanted, perm, column[a], column[b], grad_from[a], grad_from[b], width
        )
        got = exchange_plane(sent.reshape(LANES, pair, width + hidden))
        got = got.reshape(group_rows, width + hidden)
        back, grad = expert(got, full_w)
        picks.append(pick)
        xs.append(got)
        grads.append(grad)
        backs.append(back)

    going = {}
    for n in BACK:
        back = exchange_plane(backs[n].reshape(LANES, pair, width))
        back = back.reshape(group_rows, width)
        for i, s in enumerate(GROUPS[n]):
            sign = 1 if s > 0 else -1
            part = dot(picks[n][:, i * tok_dev : (i + 1) * tok_dev], back, ((0,), (0,)))
            if s == 0:
                home = part
                continue
            if sign in going:
                part = part + going[sign].astype(f32)
            going[sign] = shifted(part.astype(bf16), sign)
    token_grad = (home + going[1].astype(f32) + going[-1].astype(f32)).astype(bf16)

    grad_rows = jnp.concatenate(grads, axis=0)
    me_ref = me.astype(i32).reshape(1)
    to_core = weight_grad(me_ref, xs, grad_rows, 1)
    from_core = swapped(to_core, "core")
    kept = weight_grad(me_ref, xs, grad_rows, 0)
    other = (kept[1].astype(f32) + from_core[1].astype(f32)).astype(bf16)
    moving = jnp.sum(jnp.where(jnp.arange(slots, dtype=i32) == here, swap_mask, 0)) == 1
    size = shard // SWAP_PARTS
    steps = []
    for s in range(SWAP_PARTS):
        at = slice(s * size, (s + 1) * size)
        from_x = swapped(other[at], "xl")
        if s > 0:
            from_x, _ = lax.optimization_barrier((from_x, stepped))
        grad = kept[0, at].astype(f32) + from_core[0, at].astype(f32) + from_x.astype(f32)
        stepped = adam_direction(grad, first_moment[0, at], second_moment[0, at])
        partner = swapped(stepped, "xh")
        steps.append(jnp.where(moving, partner, stepped))
    adam_step = jnp.concatenate(steps, axis=0)[None]
    return (token_grad, adam_step)


def solution(mesh):
    names = ("xl", "core", "xh", "y", "z")
    fine = Mesh(mesh.devices.reshape(2, 2, 2, 4, 8), names)
    dp, expert = ("xl", "core"), ("xh", "y", "z")
    in_specs = (
        P(names, None),
        P(names, None),
        P(names, None, None),
        P(),
        P(),
        P(expert, dp, None),
        P(expert, dp, None),
        P(expert, dp, None),
    )
    out_specs = (P(names, None), P(expert, dp, None))
    return jax.shard_map(step, mesh=fine, in_specs=in_specs, out_specs=out_specs, check_vma=False)
```

```python
import functools

import jax
import jax.numpy as jnp
import numpy as np
from jax import lax
from jax.experimental import pallas as pl
from jax.experimental.pallas import tpu as pltpu
from jax.sharding import Mesh, PartitionSpec as P

CAP = 12
PLANES = 8
LANES = 8
GROUPS = ((-1, 1), (3, 0, 2, -2), (-4, -3))
BACK = ((1, 0), (2, 0), (1, 1), (0, 0))
SWAP_PARTS = 2


def adam_kernel(a, b, c, first, second, out):
    grad = a[...].astype(jnp.float32) + b[...].astype(jnp.float32) + c[...].astype(jnp.float32)
    first_new = 0.9 * first[0] + 0.1 * grad
    second_new = 0.95 * second[0] + 0.05 * grad * grad
    out[...] = (first_new / (jnp.sqrt(second_new) + 1e-08)).astype(out.dtype)


def adam_direction(own, from_core, from_x, first, second, part):
    rows, hidden = from_x.shape
    bn = 64
    skip = part * (rows // bn)
    here = pl.BlockSpec((bn, hidden), lambda i: (i + skip, 0))
    short = pl.BlockSpec((bn, hidden), lambda i: (i, 0))
    moment = pl.BlockSpec((1, bn, hidden), lambda i: (0, i + skip, 0))
    return pl.pallas_call(
        adam_kernel,
        grid=(rows // bn,),
        in_specs=[here, here, short, moment, moment],
        out_specs=short,
        out_shape=jax.ShapeDtypeStruct((rows, hidden), jnp.bfloat16),
        cost_estimate=pl.CostEstimate(
            flops=12 * rows * hidden, bytes_accessed=16 * rows * hidden, transcendentals=0
        ),
        name="adam",
    )(own, from_core, from_x, first, second)


def dot(a, b, contract=((1,), (0,))):
    return lax.dot_general(a, b, (contract, ((), ())), preferred_element_type=jnp.float32)


def exchange_plane(block):
    groups = [
        [((low ^ high) * 2 + high) * 4 + y for high in range(2) for y in range(4)]
        for low in range(2)
    ]
    return lax.all_to_all(block, ("xl", "xh", "y"), 0, 0, axis_index_groups=groups, tiled=True)


def swapped(block, axis):
    return lax.ppermute(block, axis, [(0, 1), (1, 0)])


def shifted(block, by):
    return lax.ppermute(block, "z", [(i, (i + by) % PLANES) for i in range(PLANES)])


def dw_kernel(count, me, *refs):
    xs, g, out, joined = refs[:count], refs[count], refs[count + 1], refs[count + 2]
    at = 0
    for x in xs:
        joined[pl.ds(at, x.shape[0]), :] = x[...]
        at += x.shape[0]
    out[...] = dot(joined[...], g[...], ((0,), (0,))).astype(out.dtype)


def weight_grad(me, xs, g, other):
    rows, hidden = g.shape
    width = xs[0].shape[1] - hidden
    shard = width // 4
    bn = 256
    per = shard // bn
    spec = [
        pl.BlockSpec((x.shape[0], bn), lambda i, m: (0, jnp.bitwise_xor(m[0], other) * per + i))
        for x in xs
    ]
    return pl.pallas_call(
        functools.partial(dw_kernel, len(xs)),
        grid_spec=pltpu.PrefetchScalarGridSpec(
            num_scalar_prefetch=1,
            grid=(per,),
            in_specs=spec + [pl.BlockSpec(g.shape, lambda i, m: (0, 0))],
            out_specs=pl.BlockSpec((bn, hidden), lambda i, m: (i, 0)),
            scratch_shapes=[pltpu.VMEM((rows, bn), jnp.bfloat16)],
        ),
        out_shape=jax.ShapeDtypeStruct((shard, hidden), jnp.bfloat16),
        cost_estimate=pl.CostEstimate(
            flops=2 * rows * shard * hidden,
            bytes_accessed=2 * (rows * shard + shard * hidden + g.size),
            transcendentals=0,
        ),
    )(me, *xs, g)


def pack_kernel(count, *refs):
    choose, wanted, wide, perm = refs[:4]
    cs, gs = refs[4 : 4 + count], refs[4 + count : 4 + 2 * count]
    sent, picks = refs[4 + 2 * count], refs[5 + 2 * count : -2]
    tokens, hidden = refs[-2:]
    for i, (c, g) in enumerate(zip(cs, gs)):
        tokens[pl.ds(i * c.shape[0], c.shape[0]), :] = c[...]
        hidden[pl.ds(i * g.shape[0], g.shape[0]), :] = g[...]
    width = sent.shape[1] - hidden.shape[1]
    value = dot(choose[...], tokens[:, width:], ((1,), (1,)))
    for i, pick in enumerate(picks):
        cols = pick.shape[1]
        part = value[:, i * cols : (i + 1) * cols]
        hit = (part[:, None, :] == wanted[...][None]).astype(jnp.float32)
        pick[...] = hit.reshape(pick.shape).astype(jnp.bfloat16)
    if count == 2:
        chosen = picks[0][...]
    else:
        hit = (value[:, None, :] == wide[...][None]).astype(jnp.float32)
        chosen = hit.reshape(perm.shape[0], value.shape[1]).astype(jnp.bfloat16)
    bn = 512

    def columns(i, carry):
        at = pl.ds(pl.multiple_of(i * bn, bn), bn)
        sent[:, at] = dot(chosen, tokens[:, at]).astype(sent.dtype)
        return carry

    lax.fori_loop(0, width // bn, columns, 0)
    sent[:, width:] = dot(perm[...], hidden[...]).astype(sent.dtype)


def wanted_rank(count, tok_dev):
    q, t = np.arange(count * CAP)[:, None], np.arange(count * tok_dev)[None, :]
    return jnp.asarray(np.where(q // CAP == t // tok_dev, q % CAP + 1.0, -1.0), jnp.float32)


def pack(choose, cs, gs, width):
    count, tok_dev, hidden = len(cs), cs[0].shape[0], gs[0].shape[1]
    rows = LANES * count * CAP
    order = [
        (s * LANES + j) * CAP + r for j in range(LANES) for s in range(count) for r in range(CAP)
    ]
    source = jnp.asarray(np.array(order, np.int32))[:, None]
    perm = (source == lax.broadcasted_iota(jnp.int32, (rows, rows), 1)).astype(jnp.bfloat16)
    pick = jax.ShapeDtypeStruct((LANES * 2 * CAP, 2 * tok_dev), jnp.bfloat16)
    return pl.pallas_call(
        functools.partial(pack_kernel, count),
        out_shape=[jax.ShapeDtypeStruct((rows, width + hidden), jnp.bfloat16)]
        + [pick] * (count // 2),
        scratch_shapes=[
            pltpu.VMEM((count * tok_dev, cs[0].shape[1]), jnp.bfloat16),
            pltpu.VMEM((rows, hidden), jnp.bfloat16),
        ],
    )(choose, wanted_rank(2, tok_dev), wanted_rank(count, tok_dev), perm, *cs, *gs)


def expert_kernel(steps, x, g0, g1, g2, w, grad, *rest):
    backs, acc = rest[:-1], rest[-1]
    phase, k = pl.program_id(0), pl.program_id(1)

    @pl.when(phase == 0)
    def _():
        part = dot(x[...], w[...])

        @pl.when(k == 0)
        def _():
            acc[...] = part

        @pl.when(k > 0)
        def _():
            acc[...] += part

        @pl.when(k == steps - 1)
        def _():
            wide = g0.shape[1]
            for i, g in enumerate((g0, g1, g2)):
                at = pl.ds(i * wide, wide)
                pre = acc[:, at]
                sig = jax.nn.sigmoid(pre)
                value = g[...].astype(jnp.float32) * sig * (1.0 + pre * (1.0 - sig))
                grad[:, at] = value.astype(grad.dtype)

    @pl.when(phase == 1)
    def _():
        value = dot(grad[...], w[...], ((1,), (1,)))
        rows, kb = value.shape
        split = value.reshape(LANES, rows // LANES, kb)
        for i, back in enumerate(backs):
            piece = split[:, i * 2 * CAP : (i + 1) * 2 * CAP]
            back[...] = piece.reshape(back.shape).astype(back.dtype)


def expert(got, full_w):
    width, hidden = full_w.shape
    rows = got.shape[0]
    kb = 1024
    nk = width // kb
    third = hidden // 3
    pair_rows = LANES * 2 * CAP
    pairs = rows // pair_rows
    side = [pl.BlockSpec((rows, third), lambda p, k, i=i: (0, width // third + i)) for i in range(3)]
    return pl.pallas_call(
        functools.partial(expert_kernel, nk),
        grid=(2, nk),
        in_specs=[pl.BlockSpec((rows, kb), lambda p, k: (0, jnp.where(p == 0, k, nk - 1)))]
        + side
        + [pl.BlockSpec((kb, hidden), lambda p, k: (k, 0))],
        out_specs=[pl.BlockSpec((rows, hidden), lambda p, k: (0, 0))]
        + [pl.BlockSpec((pair_rows, kb), lambda p, k: (0, jnp.where(p == 0, 0, k)))] * pairs,
        out_shape=[jax.ShapeDtypeStruct((rows, hidden), jnp.bfloat16)]
        + [jax.ShapeDtypeStruct((pair_rows, width), jnp.bfloat16)] * pairs,
        scratch_shapes=[pltpu.VMEM((rows, hidden), jnp.float32)],
        cost_estimate=pl.CostEstimate(
            flops=4 * rows * width * hidden,
            bytes_accessed=4 * width * (hidden + rows),
            transcendentals=rows * hidden,
        ),
    )(got, got, got, got, full_w)


def step(
    tokens, token_experts, hidden_grad, held_expert, swap_mask, weight, first_moment, second_moment
):
    bf16, f32, i32 = jnp.bfloat16, jnp.float32, jnp.int32
    xl, core, xh = lax.axis_index("xl"), lax.axis_index("core"), lax.axis_index("xh")
    y, z = lax.axis_index("y"), lax.axis_index("z")
    here = (xh * 4 + y) * PLANES + z
    me = xl * 2 + core
    tok_dev, top = token_experts.shape
    width, hidden = tokens.shape[1], hidden_grad.shape[2]
    slots = held_expert.shape[0]
    pair = 2 * CAP

    w_own = weight[0]
    w_x = swapped(w_own, "xl")
    w_c = swapped(jnp.stack([w_own, w_x]), "core")
    shard = w_own.shape[0]
    full_w = jnp.zeros((width, hidden), bf16)
    for i, piece in ((0, w_own), (2, w_x), (1, w_c[0]), (3, w_c[1])):
        full_w = lax.dynamic_update_slice(full_w, piece, ((me ^ i) * shard, 0))

    same = token_experts[:, :, None] == held_expert[None, None, :]
    named = jnp.sum(same.astype(f32), axis=1).astype(bf16)
    earlier = jnp.asarray(np.tril(np.ones((tok_dev, tok_dev)), -1), bf16)
    rank = named.astype(f32) * (dot(earlier, named) + 1.0)

    marks = jnp.pad(rank.astype(bf16), ((0, 0), (0, 128 - slots)))
    own = jnp.concatenate([tokens, marks], axis=1)
    column = {0: own}
    for k in range(1, 5):
        column[-k] = shifted(column[1 - k], 1)
        if k < 4:
            column[k] = shifted(column[k - 1], -1)

    slot_p = np.arange(slots)
    ahead = jnp.bitwise_and(jnp.asarray(slot_p % PLANES, i32) - z, PLANES - 1) * (LANES * CAP)
    place = (ahead + jnp.asarray(slot_p // PLANES * CAP - 1, i32)).astype(f32)
    slot = jnp.sum(jnp.where(same, (rank + place[None, :])[:, None, :], 0.0), axis=2)
    slot = slot.astype(i32).reshape(1, tok_dev * top)
    pick_g = (lax.broadcasted_iota(i32, (slots * CAP, tok_dev * top), 0) == slot).astype(bf16)
    send_g = dot(pick_g, hidden_grad.reshape(tok_dev * top, hidden)).astype(bf16)
    send_g = send_g.reshape(PLANES, LANES * CAP, hidden)
    grad_from = {0: send_g[0]}
    for d in (1, -1, 2, -2, 4, 3, -3):
        grad_from[-d] = shifted(send_g[d % PLANES], d)

    lane_i = lax.broadcasted_iota(i32, (LANES, 128), 0)
    slot_i = lax.broadcasted_iota(i32, (LANES, 128), 1)
    choose = (slot_i == lane_i * PLANES + z).astype(bf16)
    picks, xs, grads, backs = [], [], [], []
    for group in GROUPS:
        sent, *pick = pack(choose, [column[s] for s in group], [grad_from[s] for s in group], width)
        rows = sent.shape[0]
        got = exchange_plane(sent.reshape(LANES, rows // LANES, width + hidden))
        got = got.reshape(rows, width + hidden)
        grad, *back = expert(got, full_w)
        picks.append(pick)
        xs.append(got)
        grads.append(grad)
        backs.append(back)

    going = {}
    for n, h in BACK:
        back = exchange_plane(backs[n][h].reshape(LANES, pair, width))
        back = back.reshape(LANES * pair, width)
        for i, s in enumerate(GROUPS[n][2 * h : 2 * h + 2]):
            sign = 1 if s > 0 else -1
            part = dot(picks[n][h][:, i * tok_dev : (i + 1) * tok_dev], back, ((0,), (0,)))
            if s == 0:
                home = part
                continue
            if sign in going:
                part = part + going[sign].astype(f32)
            going[sign] = shifted(part.astype(bf16), sign)
    token_grad = (home + going[1].astype(f32) + going[-1].astype(f32)).astype(bf16)

    grad_rows = jnp.concatenate(grads, axis=0)
    me_ref = me.astype(i32).reshape(1)
    block = {}
    for other in (3, 2, 1, 0):
        block[other] = weight_grad(me_ref, xs, grad_rows, other)
    from_core_x = swapped(block[3], "core")
    from_core = swapped(block[1], "core")
    other = (block[2].astype(f32) + from_core_x.astype(f32)).astype(bf16)
    moving = jnp.sum(jnp.where(jnp.arange(slots, dtype=i32) == here, swap_mask, 0)) == 1
    size = shard // SWAP_PARTS
    steps = []
    for s in range(SWAP_PARTS):
        at = slice(s * size, (s + 1) * size)
        from_x = swapped(other[at], "xl")
        stepped = adam_direction(block[0], from_core, from_x, first_moment, second_moment, s)
        partner = swapped(stepped, "xh")
        steps.append(jnp.where(moving, partner, stepped))
    adam_step = jnp.concatenate(steps, axis=0)[None]
    return (token_grad, adam_step)


def solution(mesh):
    names = ("xl", "core", "xh", "y", "z")
    fine = Mesh(mesh.devices.reshape(2, 2, 2, 4, 8), names)
    dp, expert = ("xl", "core"), ("xh", "y", "z")
    in_specs = (
        P(names, None),
        P(names, None),
        P(names, None, None),
        P(),
        P(),
        P(expert, dp, None),
        P(expert, dp, None),
        P(expert, dp, None),
    )
    out_specs = (P(names, None), P(expert, dp, None))
    return jax.shard_map(step, mesh=fine, in_specs=in_specs, out_specs=out_specs, check_vma=False)
```

```python
import functools

import jax
import jax.numpy as jnp
import numpy as np
from jax import lax
from jax.experimental import pallas as pl
from jax.experimental.pallas import tpu as pltpu
from jax.sharding import Mesh, PartitionSpec as P

CAP = 12
PLANES = 8
LANES = 8
GROUPS = ((-1, 1), (-2, 2), (-4, 3, -3, 0))
BACK = ((1, 0), (2, 0), (2, 1), (0, 0))
SWAP_PARTS = 2


def adam_kernel(a, b, c, first, second, out):
    bn = 64

    def rows(i, carry):
        at = pl.ds(pl.multiple_of(i * bn, bn), bn)
        grad = a[0, at].astype(jnp.float32) + b[0, at].astype(jnp.float32)
        grad = grad + c[at].astype(jnp.float32)
        first_new = 0.9 * first[0, at] + 0.1 * grad
        second_new = 0.95 * second[0, at] + 0.05 * grad * grad
        out[at] = (first_new / (jnp.sqrt(second_new) + 1e-08)).astype(out.dtype)
        return carry

    lax.fori_loop(0, out.shape[0] // bn, rows, 0)


def adam_direction(own, from_core, from_x, first, second, part):
    rows, hidden = from_x.shape
    bn = 256
    skip = part * (rows // bn)
    long = pl.BlockSpec((1, bn, hidden), lambda i: (0, i + skip, 0))
    short = pl.BlockSpec((bn, hidden), lambda i: (i, 0))
    return pl.pallas_call(
        adam_kernel,
        grid=(rows // bn,),
        in_specs=[long, long, short, long, long],
        out_specs=short,
        out_shape=jax.ShapeDtypeStruct((rows, hidden), jnp.bfloat16),
        cost_estimate=pl.CostEstimate(
            flops=12 * rows * hidden, bytes_accessed=16 * rows * hidden, transcendentals=0
        ),
        name="adam",
    )(own, from_core, from_x, first, second)


def dot(a, b, contract=((1,), (0,))):
    return lax.dot_general(a, b, (contract, ((), ())), preferred_element_type=jnp.float32)


def exchange_plane(block):
    groups = [
        [((low ^ high) * 2 + high) * 4 + y for high in range(2) for y in range(4)]
        for low in range(2)
    ]
    return lax.all_to_all(block, ("xl", "xh", "y"), 0, 0, axis_index_groups=groups, tiled=True)


def swapped(block, axis):
    return lax.ppermute(block, axis, [(0, 1), (1, 0)])


def shifted(block, by):
    return lax.ppermute(block, "z", [(i, (i + by) % PLANES) for i in range(PLANES)])


def dw_kernel(count, me, *refs):
    xs, g, out, joined = refs[:count], refs[count], refs[count + 1], refs[count + 2]
    at = 0
    for x in xs:
        joined[pl.ds(at, x.shape[0]), :] = x[...]
        at += x.shape[0]
    out[0] = dot(joined[...], g[...], ((0,), (0,))).astype(out.dtype)


def weight_grad(me, xs, g, odd):
    rows, hidden = g.shape
    width = xs[0].shape[1] - hidden
    shard = width // 4
    bn = 512
    per = shard // bn
    spec = [
        pl.BlockSpec(
            (x.shape[0], bn), lambda h, i, m: (0, jnp.bitwise_xor(2 * h + odd, m[0]) * per + i)
        )
        for x in xs
    ]
    return pl.pallas_call(
        functools.partial(dw_kernel, len(xs)),
        grid_spec=pltpu.PrefetchScalarGridSpec(
            num_scalar_prefetch=1,
            grid=(2, per),
            in_specs=spec + [pl.BlockSpec(g.shape, lambda h, i, m: (0, 0))],
            out_specs=pl.BlockSpec((1, bn, hidden), lambda h, i, m: (h, i, 0)),
            scratch_shapes=[pltpu.VMEM((rows, bn), jnp.bfloat16)],
        ),
        out_shape=jax.ShapeDtypeStruct((2, shard, hidden), jnp.bfloat16),
        cost_estimate=pl.CostEstimate(
            flops=4 * rows * shard * hidden,
            bytes_accessed=2 * (2 * rows * shard + 2 * shard * hidden + g.size),
            transcendentals=0,
        ),
    )(me, *xs, g)


def pack_kernel(count, *refs):
    choose, wanted, wide, perm = refs[:4]
    cs, gs = refs[4 : 4 + count], refs[4 + count : 4 + 2 * count]
    sent, picks = refs[4 + 2 * count], refs[5 + 2 * count : -2]
    tokens, hidden = refs[-2:]
    for i, (c, g) in enumerate(zip(cs, gs)):
        tokens[pl.ds(i * c.shape[0], c.shape[0]), :] = c[...]
        hidden[pl.ds(i * g.shape[0], g.shape[0]), :] = g[...]
    width = sent.shape[1] - hidden.shape[1]
    value = dot(choose[...], tokens[:, width:], ((1,), (1,)))
    for i, pick in enumerate(picks):
        cols = pick.shape[1]
        part = value[:, i * cols : (i + 1) * cols]
        hit = (part[:, None, :] == wanted[...][None]).astype(jnp.float32)
        pick[...] = hit.reshape(pick.shape).astype(jnp.bfloat16)
    if count == 2:
        chosen = picks[0][...]
    else:
        hit = (value[:, None, :] == wide[...][None]).astype(jnp.float32)
        chosen = hit.reshape(perm.shape[0], value.shape[1]).astype(jnp.bfloat16)
    bn = 512

    def columns(i, carry):
        at = pl.ds(pl.multiple_of(i * bn, bn), bn)
        sent[:, at] = dot(chosen, tokens[:, at]).astype(sent.dtype)
        return carry

    lax.fori_loop(0, width // bn, columns, 0)
    sent[:, width:] = dot(perm[...], hidden[...]).astype(sent.dtype)


def wanted_rank(count, tok_dev):
    q, t = np.arange(count * CAP)[:, None], np.arange(count * tok_dev)[None, :]
    return jnp.asarray(np.where(q // CAP == t // tok_dev, q % CAP + 1.0, -1.0), jnp.float32)


def pack(choose, cs, gs, width):
    count, tok_dev, hidden = len(cs), cs[0].shape[0], gs[0].shape[1]
    rows = LANES * count * CAP
    order = [
        (s * LANES + j) * CAP + r for j in range(LANES) for s in range(count) for r in range(CAP)
    ]
    source = jnp.asarray(np.array(order, np.int32))[:, None]
    perm = (source == lax.broadcasted_iota(jnp.int32, (rows, rows), 1)).astype(jnp.bfloat16)
    pick = jax.ShapeDtypeStruct((LANES * 2 * CAP, 2 * tok_dev), jnp.bfloat16)
    return pl.pallas_call(
        functools.partial(pack_kernel, count),
        out_shape=[jax.ShapeDtypeStruct((rows, width + hidden), jnp.bfloat16)]
        + [pick] * (count // 2),
        scratch_shapes=[
            pltpu.VMEM((count * tok_dev, cs[0].shape[1]), jnp.bfloat16),
            pltpu.VMEM((rows, hidden), jnp.bfloat16),
        ],
    )(choose, wanted_rank(2, tok_dev), wanted_rank(count, tok_dev), perm, *cs, *gs)


def expert_kernel(steps, x, g0, g1, g2, w, grad, *rest):
    backs, acc = rest[:-1], rest[-1]
    phase, k = pl.program_id(0), pl.program_id(1)

    @pl.when(phase == 0)
    def _():
        part = dot(x[...], w[...])

        @pl.when(k == 0)
        def _():
            acc[...] = part

        @pl.when(k > 0)
        def _():
            acc[...] += part

        @pl.when(k == steps - 1)
        def _():
            wide = g0.shape[1]
            for i, g in enumerate((g0, g1, g2)):
                at = pl.ds(i * wide, wide)
                pre = acc[:, at]
                sig = jax.nn.sigmoid(pre)
                value = g[...].astype(jnp.float32) * sig * (1.0 + pre * (1.0 - sig))
                grad[:, at] = value.astype(grad.dtype)

    @pl.when(phase == 1)
    def _():
        value = dot(grad[...], w[...], ((1,), (1,)))
        rows, kb = value.shape
        split = value.reshape(LANES, rows // LANES, kb)
        for i, back in enumerate(backs):
            piece = split[:, i * 2 * CAP : (i + 1) * 2 * CAP]
            back[...] = piece.reshape(back.shape).astype(back.dtype)


def expert(got, full_w):
    width, hidden = full_w.shape
    rows = got.shape[0]
    kb = 1024
    nk = width // kb
    third = hidden // 3
    pair_rows = LANES * 2 * CAP
    pairs = rows // pair_rows
    side = [pl.BlockSpec((rows, third), lambda p, k, i=i: (0, width // third + i)) for i in range(3)]
    return pl.pallas_call(
        functools.partial(expert_kernel, nk),
        grid=(2, nk),
        in_specs=[pl.BlockSpec((rows, kb), lambda p, k: (0, jnp.where(p == 0, k, nk - 1)))]
        + side
        + [pl.BlockSpec((kb, hidden), lambda p, k: (k, 0))],
        out_specs=[pl.BlockSpec((rows, hidden), lambda p, k: (0, 0))]
        + [pl.BlockSpec((pair_rows, kb), lambda p, k: (0, jnp.where(p == 0, 0, k)))] * pairs,
        out_shape=[jax.ShapeDtypeStruct((rows, hidden), jnp.bfloat16)]
        + [jax.ShapeDtypeStruct((pair_rows, width), jnp.bfloat16)] * pairs,
        scratch_shapes=[pltpu.VMEM((rows, hidden), jnp.float32)],
        cost_estimate=pl.CostEstimate(
            flops=4 * rows * width * hidden,
            bytes_accessed=4 * width * (hidden + rows),
            transcendentals=rows * hidden,
        ),
    )(got, got, got, got, full_w)


def step(
    tokens, token_experts, hidden_grad, held_expert, swap_mask, weight, first_moment, second_moment
):
    bf16, f32, i32 = jnp.bfloat16, jnp.float32, jnp.int32
    xl, core, xh = lax.axis_index("xl"), lax.axis_index("core"), lax.axis_index("xh")
    y, z = lax.axis_index("y"), lax.axis_index("z")
    here = (xh * 4 + y) * PLANES + z
    me = xl * 2 + core
    tok_dev, top = token_experts.shape
    width, hidden = tokens.shape[1], hidden_grad.shape[2]
    slots = held_expert.shape[0]
    pair = 2 * CAP

    w_own = weight[0]
    w_x = swapped(w_own, "xl")
    w_c = swapped(jnp.stack([w_own, w_x]), "core")
    shard = w_own.shape[0]
    full_w = jnp.zeros((width, hidden), bf16)
    for i, piece in ((0, w_own), (2, w_x), (1, w_c[0]), (3, w_c[1])):
        full_w = lax.dynamic_update_slice(full_w, piece, ((me ^ i) * shard, 0))

    same = token_experts[:, :, None] == held_expert[None, None, :]
    named = jnp.sum(same.astype(f32), axis=1).astype(bf16)
    earlier = jnp.asarray(np.tril(np.ones((tok_dev, tok_dev)), -1), bf16)
    rank = named.astype(f32) * (dot(earlier, named) + 1.0)

    marks = jnp.pad(rank.astype(bf16), ((0, 0), (0, 128 - slots)))
    own = jnp.concatenate([tokens, marks], axis=1)
    column = {0: own}
    for k in range(1, 5):
        column[-k] = shifted(column[1 - k], 1)
        if k < 4:
            column[k] = shifted(column[k - 1], -1)

    slot_p = np.arange(slots)
    ahead = jnp.bitwise_and(jnp.asarray(slot_p % PLANES, i32) - z, PLANES - 1) * (LANES * CAP)
    place = (ahead + jnp.asarray(slot_p // PLANES * CAP - 1, i32)).astype(f32)
    slot = jnp.sum(jnp.where(same, (rank + place[None, :])[:, None, :], 0.0), axis=2)
    slot = slot.astype(i32).reshape(1, tok_dev * top)
    pick_g = (lax.broadcasted_iota(i32, (slots * CAP, tok_dev * top), 0) == slot).astype(bf16)
    send_g = dot(pick_g, hidden_grad.reshape(tok_dev * top, hidden)).astype(bf16)
    send_g = send_g.reshape(PLANES, LANES * CAP, hidden)
    grad_from = {0: send_g[0]}
    for d in (1, -1, 2, -2, 4, 3, -3):
        grad_from[-d] = shifted(send_g[d % PLANES], d)

    lane_i = lax.broadcasted_iota(i32, (LANES, 128), 0)
    slot_i = lax.broadcasted_iota(i32, (LANES, 128), 1)
    choose = (slot_i == lane_i * PLANES + z).astype(bf16)
    picks, xs, grads, backs = [], [], [], []
    for group in GROUPS:
        sent, *pick = pack(choose, [column[s] for s in group], [grad_from[s] for s in group], width)
        rows = sent.shape[0]
        got = exchange_plane(sent.reshape(LANES, rows // LANES, width + hidden))
        got = got.reshape(rows, width + hidden)
        grad, *back = expert(got, full_w)
        picks.append(pick)
        xs.append(got)
        grads.append(grad)
        backs.append(back)

    part = {}
    for n, h in BACK:
        back = exchange_plane(backs[n][h].reshape(LANES, pair, width))
        back = back.reshape(LANES * pair, width)
        for i, s in enumerate(GROUPS[n][2 * h : 2 * h + 2]):
            mine = picks[n][h][:, i * tok_dev : (i + 1) * tok_dev]
            part[s] = dot(mine, back, ((0,), (0,)))
    arrived = []
    for far, sign in ((-4, 1), (3, -1)):
        going = None
        for s in range(far, 0, sign):
            total = part[s] if going is None else part[s] + going.astype(f32)
            going = shifted(total.astype(bf16), -sign)
        arrived.append(going.astype(f32))
    token_grad = (part[0] + arrived[0] + arrived[1]).astype(bf16)

    grad_rows = jnp.concatenate(grads, axis=0)
    me_ref = me.astype(i32).reshape(1)
    to_core = weight_grad(me_ref, xs, grad_rows, 1)
    from_core = swapped(to_core, "core")
    kept = weight_grad(me_ref, xs, grad_rows, 0)
    other = (kept[1].astype(f32) + from_core[1].astype(f32)).astype(bf16)
    moving = jnp.sum(jnp.where(jnp.arange(slots, dtype=i32) == here, swap_mask, 0)) == 1
    size = shard // SWAP_PARTS
    steps = []
    for s in range(SWAP_PARTS):
        at = slice(s * size, (s + 1) * size)
        from_x = swapped(other[at], "xl")
        stepped = adam_direction(kept, from_core, from_x, first_moment, second_moment, s)
        partner = swapped(stepped, "xh")
        steps.append(jnp.where(moving, partner, stepped))
    adam_step = jnp.concatenate(steps, axis=0)[None]
    return (token_grad, adam_step)


def solution(mesh):
    names = ("xl", "core", "xh", "y", "z")
    fine = Mesh(mesh.devices.reshape(2, 2, 2, 4, 8), names)
    dp, expert = ("xl", "core"), ("xh", "y", "z")
    in_specs = (
        P(names, None),
        P(names, None),
        P(names, None, None),
        P(),
        P(),
        P(expert, dp, None),
        P(expert, dp, None),
        P(expert, dp, None),
    )
    out_specs = (P(names, None), P(expert, dp, None))
    return jax.shard_map(step, mesh=fine, in_specs=in_specs, out_specs=out_specs, check_vma=False)
```

```python
import functools

import jax
import jax.numpy as jnp
import numpy as np
from jax import lax
from jax.experimental import pallas as pl
from jax.experimental.pallas import tpu as pltpu
from jax.sharding import Mesh, PartitionSpec as P

CAP = 12
PLANES = 8
LANES = 8
GROUPS = ((-1, 1), (-2, 2), (-4, 3, -3, 0))
BACK = ((1, 0), (2, 0), (2, 1), (0, 0))
SWAP_PARTS = (5, 3)


def adam_kernel(a, b, c, first, second, out):
    bn = 64

    def rows(i, carry):
        at = pl.ds(pl.multiple_of(i * bn, bn), bn)
        grad = a[0, at].astype(jnp.float32) + b[0, at].astype(jnp.float32)
        grad = grad + c[at].astype(jnp.float32)
        first_new = 0.9 * first[0, at] + 0.1 * grad
        second_new = 0.95 * second[0, at] + 0.05 * grad * grad
        out[at] = (first_new / (jnp.sqrt(second_new) + 1e-08)).astype(out.dtype)
        return carry

    lax.fori_loop(0, out.shape[0] // bn, rows, 0)


def adam_direction(own, from_core, from_x, first, second, start):
    rows, hidden = from_x.shape
    bn = 128
    skip = start // bn
    long = pl.BlockSpec((1, bn, hidden), lambda i: (0, i + skip, 0))
    short = pl.BlockSpec((bn, hidden), lambda i: (i, 0))
    return pl.pallas_call(
        adam_kernel,
        grid=(rows // bn,),
        in_specs=[long, long, short, long, long],
        out_specs=short,
        out_shape=jax.ShapeDtypeStruct((rows, hidden), jnp.bfloat16),
        cost_estimate=pl.CostEstimate(
            flops=12 * rows * hidden, bytes_accessed=16 * rows * hidden, transcendentals=0
        ),
        name="adam",
    )(own, from_core, from_x, first, second)


def dot(a, b, contract=((1,), (0,))):
    return lax.dot_general(a, b, (contract, ((), ())), preferred_element_type=jnp.float32)


def exchange_plane(block):
    groups = [
        [((low ^ high) * 2 + high) * 4 + y for high in range(2) for y in range(4)]
        for low in range(2)
    ]
    return lax.all_to_all(block, ("xl", "xh", "y"), 0, 0, axis_index_groups=groups, tiled=True)


def swapped(block, axis):
    return lax.ppermute(block, axis, [(0, 1), (1, 0)])


def shifted(block, by):
    return lax.ppermute(block, "z", [(i, (i + by) % PLANES) for i in range(PLANES)])


def dw_kernel(count, me, *refs):
    xs, g, out, joined = refs[:count], refs[count], refs[count + 1], refs[count + 2]
    at = 0
    for x in xs:
        joined[pl.ds(at, x.shape[0]), :] = x[...]
        at += x.shape[0]
    out[0] = dot(joined[...], g[...], ((0,), (0,))).astype(out.dtype)


def weight_grad(me, xs, g, odd):
    rows, hidden = g.shape
    width = xs[0].shape[1] - hidden
    shard = width // 4
    bn = 512
    per = shard // bn
    spec = [
        pl.BlockSpec(
            (x.shape[0], bn), lambda h, i, m: (0, jnp.bitwise_xor(2 * h + odd, m[0]) * per + i)
        )
        for x in xs
    ]
    return pl.pallas_call(
        functools.partial(dw_kernel, len(xs)),
        grid_spec=pltpu.PrefetchScalarGridSpec(
            num_scalar_prefetch=1,
            grid=(2, per),
            in_specs=spec + [pl.BlockSpec(g.shape, lambda h, i, m: (0, 0))],
            out_specs=pl.BlockSpec((1, bn, hidden), lambda h, i, m: (h, i, 0)),
            scratch_shapes=[pltpu.VMEM((rows, bn), jnp.bfloat16)],
        ),
        out_shape=jax.ShapeDtypeStruct((2, shard, hidden), jnp.bfloat16),
        cost_estimate=pl.CostEstimate(
            flops=4 * rows * shard * hidden,
            bytes_accessed=2 * (2 * rows * shard + 2 * shard * hidden + g.size),
            transcendentals=0,
        ),
    )(me, *xs, g)


def pack_kernel(count, *refs):
    choose, wanted, wide, perm = refs[:4]
    cs, gs = refs[4 : 4 + count], refs[4 + count : 4 + 2 * count]
    sent, picks = refs[4 + 2 * count], refs[5 + 2 * count : -2]
    tokens, hidden = refs[-2:]
    for i, (c, g) in enumerate(zip(cs, gs)):
        tokens[pl.ds(i * c.shape[0], c.shape[0]), :] = c[...]
        hidden[pl.ds(i * g.shape[0], g.shape[0]), :] = g[...]
    width = sent.shape[1] - hidden.shape[1]
    value = dot(choose[...], tokens[:, width:], ((1,), (1,)))
    for i, pick in enumerate(picks):
        cols = pick.shape[1]
        part = value[:, i * cols : (i + 1) * cols]
        hit = (part[:, None, :] == wanted[...][None]).astype(jnp.float32)
        pick[...] = hit.reshape(pick.shape).astype(jnp.bfloat16)
    if count == 2:
        chosen = picks[0][...]
    else:
        hit = (value[:, None, :] == wide[...][None]).astype(jnp.float32)
        chosen = hit.reshape(perm.shape[0], value.shape[1]).astype(jnp.bfloat16)
    bn = 512

    def columns(i, carry):
        at = pl.ds(pl.multiple_of(i * bn, bn), bn)
        sent[:, at] = dot(chosen, tokens[:, at]).astype(sent.dtype)
        return carry

    lax.fori_loop(0, width // bn, columns, 0)
    sent[:, width:] = dot(perm[...], hidden[...]).astype(sent.dtype)


def wanted_rank(count, tok_dev):
    q, t = np.arange(count * CAP)[:, None], np.arange(count * tok_dev)[None, :]
    return jnp.asarray(np.where(q // CAP == t // tok_dev, q % CAP + 1.0, -1.0), jnp.float32)


def pack(choose, cs, gs, width):
    count, tok_dev, hidden = len(cs), cs[0].shape[0], gs[0].shape[1]
    rows = LANES * count * CAP
    order = [
        (s * LANES + j) * CAP + r for j in range(LANES) for s in range(count) for r in range(CAP)
    ]
    source = jnp.asarray(np.array(order, np.int32))[:, None]
    perm = (source == lax.broadcasted_iota(jnp.int32, (rows, rows), 1)).astype(jnp.bfloat16)
    pick = jax.ShapeDtypeStruct((LANES * 2 * CAP, 2 * tok_dev), jnp.bfloat16)
    return pl.pallas_call(
        functools.partial(pack_kernel, count),
        out_shape=[jax.ShapeDtypeStruct((rows, width + hidden), jnp.bfloat16)]
        + [pick] * (count // 2),
        scratch_shapes=[
            pltpu.VMEM((count * tok_dev, cs[0].shape[1]), jnp.bfloat16),
            pltpu.VMEM((rows, hidden), jnp.bfloat16),
        ],
    )(choose, wanted_rank(2, tok_dev), wanted_rank(count, tok_dev), perm, *cs, *gs)


def expert_kernel(steps, x, g0, g1, g2, w, grad, *rest):
    backs, acc = rest[:-1], rest[-1]
    phase, k = pl.program_id(0), pl.program_id(1)

    @pl.when(phase == 0)
    def _():
        part = dot(x[...], w[...])

        @pl.when(k == 0)
        def _():
            acc[...] = part

        @pl.when(k > 0)
        def _():
            acc[...] += part

        @pl.when(k == steps - 1)
        def _():
            wide = g0.shape[1]
            for i, g in enumerate((g0, g1, g2)):
                at = pl.ds(i * wide, wide)
                pre = acc[:, at]
                sig = jax.nn.sigmoid(pre)
                value = g[...].astype(jnp.float32) * sig * (1.0 + pre * (1.0 - sig))
                grad[:, at] = value.astype(grad.dtype)

    @pl.when(phase == 1)
    def _():
        value = dot(grad[...], w[...], ((1,), (1,)))
        rows, kb = value.shape
        split = value.reshape(LANES, rows // LANES, kb)
        for i, back in enumerate(backs):
            piece = split[:, i * 2 * CAP : (i + 1) * 2 * CAP]
            back[...] = piece.reshape(back.shape).astype(back.dtype)


def expert(got, full_w):
    width, hidden = full_w.shape
    rows = got.shape[0]
    kb = 1024
    nk = width // kb
    third = hidden // 3
    pair_rows = LANES * 2 * CAP
    pairs = rows // pair_rows
    side = [pl.BlockSpec((rows, third), lambda p, k, i=i: (0, width // third + i)) for i in range(3)]
    return pl.pallas_call(
        functools.partial(expert_kernel, nk),
        grid=(2, nk),
        in_specs=[pl.BlockSpec((rows, kb), lambda p, k: (0, jnp.where(p == 0, k, nk - 1)))]
        + side
        + [pl.BlockSpec((kb, hidden), lambda p, k: (k, 0))],
        out_specs=[pl.BlockSpec((rows, hidden), lambda p, k: (0, 0))]
        + [pl.BlockSpec((pair_rows, kb), lambda p, k: (0, jnp.where(p == 0, 0, k)))] * pairs,
        out_shape=[jax.ShapeDtypeStruct((rows, hidden), jnp.bfloat16)]
        + [jax.ShapeDtypeStruct((pair_rows, width), jnp.bfloat16)] * pairs,
        scratch_shapes=[pltpu.VMEM((rows, hidden), jnp.float32)],
        cost_estimate=pl.CostEstimate(
            flops=4 * rows * width * hidden,
            bytes_accessed=4 * width * (hidden + rows),
            transcendentals=rows * hidden,
        ),
    )(got, got, got, got, full_w)


def step(
    tokens, token_experts, hidden_grad, held_expert, swap_mask, weight, first_moment, second_moment
):
    bf16, f32, i32 = jnp.bfloat16, jnp.float32, jnp.int32
    xl, core, xh = lax.axis_index("xl"), lax.axis_index("core"), lax.axis_index("xh")
    y, z = lax.axis_index("y"), lax.axis_index("z")
    here = (xh * 4 + y) * PLANES + z
    me = xl * 2 + core
    tok_dev, top = token_experts.shape
    width, hidden = tokens.shape[1], hidden_grad.shape[2]
    slots = held_expert.shape[0]
    pair = 2 * CAP

    w_own = weight[0]
    w_x = swapped(w_own, "xl")
    w_c = swapped(jnp.stack([w_own, w_x]), "core")
    shard = w_own.shape[0]
    full_w = jnp.zeros((width, hidden), bf16)
    for i, piece in ((0, w_own), (2, w_x), (1, w_c[0]), (3, w_c[1])):
        full_w = lax.dynamic_update_slice(full_w, piece, ((me ^ i) * shard, 0))

    same = token_experts[:, :, None] == held_expert[None, None, :]
    named = jnp.sum(same.astype(f32), axis=1).astype(bf16)
    earlier = jnp.asarray(np.tril(np.ones((tok_dev, tok_dev)), -1), bf16)
    rank = named.astype(f32) * (dot(earlier, named) + 1.0)

    marks = jnp.pad(rank.astype(bf16), ((0, 0), (0, 128 - slots)))
    own = jnp.concatenate([tokens, marks], axis=1)
    column = {0: own}
    for k in range(1, 5):
        column[-k] = shifted(column[1 - k], 1)
        if k < 4:
            column[k] = shifted(column[k - 1], -1)

    slot_p = np.arange(slots)
    ahead = jnp.bitwise_and(jnp.asarray(slot_p % PLANES, i32) - z, PLANES - 1) * (LANES * CAP)
    place = (ahead + jnp.asarray(slot_p // PLANES * CAP - 1, i32)).astype(f32)
    slot = jnp.sum(jnp.where(same, (rank + place[None, :])[:, None, :], 0.0), axis=2)
    slot = slot.astype(i32).reshape(1, tok_dev * top)
    pick_g = (lax.broadcasted_iota(i32, (slots * CAP, tok_dev * top), 0) == slot).astype(bf16)
    send_g = dot(pick_g, hidden_grad.reshape(tok_dev * top, hidden)).astype(bf16)
    send_g = send_g.reshape(PLANES, LANES * CAP, hidden)
    grad_from = {0: send_g[0]}
    for d in (1, -1, 2, -2, 4, 3, -3):
        grad_from[-d] = shifted(send_g[d % PLANES], d)

    lane_i = lax.broadcasted_iota(i32, (LANES, 128), 0)
    slot_i = lax.broadcasted_iota(i32, (LANES, 128), 1)
    choose = (slot_i == lane_i * PLANES + z).astype(bf16)
    picks, xs, grads, backs = [], [], [], []
    for group in GROUPS:
        sent, *pick = pack(choose, [column[s] for s in group], [grad_from[s] for s in group], width)
        rows = sent.shape[0]
        got = exchange_plane(sent.reshape(LANES, rows // LANES, width + hidden))
        got = got.reshape(rows, width + hidden)
        grad, *back = expert(got, full_w)
        picks.append(pick)
        xs.append(got)
        grads.append(grad)
        backs.append(back)

    part = {}
    for n, h in BACK:
        back = exchange_plane(backs[n][h].reshape(LANES, pair, width))
        back = back.reshape(LANES * pair, width)
        for i, s in enumerate(GROUPS[n][2 * h : 2 * h + 2]):
            mine = picks[n][h][:, i * tok_dev : (i + 1) * tok_dev]
            part[s] = dot(mine, back, ((0,), (0,)))
    arrived = []
    for far, sign in ((-4, 1), (3, -1)):
        going = None
        for s in range(far, 0, sign):
            total = part[s] if going is None else part[s] + going.astype(f32)
            going = shifted(total.astype(bf16), -sign)
        arrived.append(going.astype(f32))
    token_grad = (part[0] + arrived[0] + arrived[1]).astype(bf16)

    grad_rows = jnp.concatenate(grads, axis=0)
    me_ref = me.astype(i32).reshape(1)
    to_core = weight_grad(me_ref, xs, grad_rows, 1)
    from_core = swapped(to_core, "core")
    kept = weight_grad(me_ref, xs, grad_rows, 0)
    other = (kept[1].astype(f32) + from_core[1].astype(f32)).astype(bf16)
    moving = jnp.sum(jnp.where(jnp.arange(slots, dtype=i32) == here, swap_mask, 0)) == 1
    steps = []
    start = 0
    for eighths in SWAP_PARTS:
        at = slice(start, start + shard // 8 * eighths)
        from_x = swapped(other[at], "xl")
        stepped = adam_direction(kept, from_core, from_x, first_moment, second_moment, start)
        start = at.stop
        partner = swapped(stepped, "xh")
        steps.append(jnp.where(moving, partner, stepped))
    adam_step = jnp.concatenate(steps, axis=0)[None]
    return (token_grad, adam_step)


def solution(mesh):
    names = ("xl", "core", "xh", "y", "z")
    fine = Mesh(mesh.devices.reshape(2, 2, 2, 4, 8), names)
    dp, expert = ("xl", "core"), ("xh", "y", "z")
    in_specs = (
        P(names, None),
        P(names, None),
        P(names, None, None),
        P(),
        P(),
        P(expert, dp, None),
        P(expert, dp, None),
        P(expert, dp, None),
    )
    out_specs = (P(names, None), P(expert, dp, None))
    return jax.shard_map(step, mesh=fine, in_specs=in_specs, out_specs=out_specs, check_vma=False)
```
